128 devices in a mesh: dp: 8 (over y_lo, z), tensor: 16 (over x, y_hi, core).
Axes of the slice: x: 4, y: 4 (y_hi: 2, y_lo: 2; y = y_hi * 2 + y_lo), z: 4, core: 2. Of those that a mesh axis runs over, the one named last changes fastest.
Arguments:
- tokens: bfloat16 [1024, 4096], P(('dp', 'tensor')), may hold values from -6 to 6
- out_grad: bfloat16 [1024, 4096], P(('dp', 'tensor')), may hold values from -6 to 6
- gate_blocks: bfloat16 [1792, 128, 128], P('tensor'), may hold values from -0.125 to 0.125
- up_blocks: bfloat16 [1792, 128, 128], P('tensor'), may hold values from -0.125 to 0.125
- down_blocks: bfloat16 [1792, 128, 128], P('tensor'), may hold values from -0.0625 to 0.0625
- gate_index: int32 [16, 112], P('tensor'), may hold values from 0 to 223, as said below
- up_index: int32 [16, 112], P('tensor'), may hold values from 0 to 223, as said below
- down_index: int32 [16, 112], P('tensor'), may hold values from 0 to 223, as said below
- gate_slot: int32 [16, 112], P('tensor'), may hold values from 0 to 135, as said below
- up_slot: int32 [16, 112], P('tensor'), may hold values from 0 to 135, as said below
- down_slot: int32 [16, 112], P('tensor'), may hold values from 0 to 135, as said below
Outputs:
- layer_out: bfloat16 [1024, 4096], P(('dp', 'tensor'))
- token_grad: bfloat16 [1024, 4096], P(('dp', 'tensor'))
- gate_grad: float32 [16, 136, 128, 128], P('tensor', 'dp')
- up_grad: float32 [16, 136, 128, 128], P('tensor', 'dp')
- down_grad: float32 [16, 136, 128, 128], P('tensor', 'dp')
The draws below stay inside these ranges and needn't reach their ends.
Inputs may be any that keep to these rules, and one draw needn't show every extreme that they name: `gate_index`: each row holds 112 distinct block numbers in increasing order. `up_index`: each row holds 112 distinct block numbers in increasing order. `down_index`: each row holds 112 distinct block numbers in increasing order. `gate_slot`: each row's 112 values are distinct; value v is slot v % 17 of data group v // 17; in every row some data group receives exactly 17 blocks. `up_slot`: each row's 112 values are distinct; value v is slot v % 17 of data group v // 17; in every row some data group receives exactly 17 blocks. `down_slot`: each row's 112 values are distinct; value v is slot v % 17 of data group v // 17; in every row some data group receives exactly 17 blocks.
All inputs are finite; a program needn't handle non-finite values.
Results may differ from the reference program's by a relative error of at most 0.019.
Values may be sent and summed in bfloat16 or wider, within the bound.
A program may use at most 192 MiB of HBM per device.

```python
import math
import jax
import jax.numpy as jnp
from jax import lax

D = 4096
FF = 14336
BLK = 128
GROUP_TOK = 128
TOKENS = 1024
FF_DEV = 896
NBLK = 224
KB = 112
CAP = 17
N_DP = 8
N_TENSOR = 16


def kept_lists(key):
    keys = jax.random.split(key, N_TENSOR)

    def one_row(row_key):
        order = jax.random.permutation(row_key, NBLK)
        return jnp.sort(order[:KB])
    return jax.vmap(one_row)(keys).astype(jnp.int32)


def slot_lists(key):
    keys = jax.random.split(key, N_TENSOR)
    slot_total = N_DP * CAP

    def one_row(row_key):
        first_key, second_key, third_key = jax.random.split(row_key, 3)
        fullest = jax.random.randint(first_key, (), 0, N_DP)
        ranks = jax.random.permutation(second_key, slot_total)
        slot_ids = jnp.arange(slot_total, dtype=jnp.int32)
        scores = jnp.where(slot_ids // CAP == fullest, ranks, ranks + slot_total)
        ordered = jnp.argsort(scores, stable=True)
        return jax.random.permutation(third_key, ordered[:KB])
    return jax.vmap(one_row)(keys).astype(jnp.int32)


def draw_gate_index(key, part):
    return kept_lists(jax.random.fold_in(key, 101))


def draw_up_index(key, part):
    return kept_lists(jax.random.fold_in(key, 202))


def draw_down_index(key, part):
    return kept_lists(jax.random.fold_in(key, 303))


def draw_gate_slot(key, part):
    return slot_lists(jax.random.fold_in(key, 404))


def draw_up_slot(key, part):
    return slot_lists(jax.random.fold_in(key, 505))


def draw_down_slot(key, part):
    return slot_lists(jax.random.fold_in(key, 606))


def shard_levels(rng, extent, cuts, least, top_value):
    def one(dim, parts):
        draws = jax.random.uniform(jax.random.fold_in(jax.random.fold_in(rng, 6), dim), (parts,), jnp.float32, least / len(cuts), top_value / len(cuts))
        return jnp.repeat(jnp.exp(draws), extent[dim] // parts).reshape((-1,) + (1,) * (len(extent) - dim - 1))

    gain = one(*cuts[0])
    for cut in cuts[1:]:
        gain = gain * one(*cut)
    return gain


def centred(own_key, shape, deviation, limit, pieces=(), kind=jnp.bfloat16):
    array = jax.random.normal(own_key, shape, jnp.float32) * deviation
    if len(pieces) > 0:
        array = shard_levels(own_key, shape, pieces, -0.22, 0.18) * array
    return jnp.clip(array, min=-limit, max=limit).astype(kind)


def setup_inputs(seed: int = 0) -> dict:
    arg_keys = jax.random.split(jax.random.key(seed), 12)
    return {
        "tokens": centred(arg_keys[0], (TOKENS, D), 1.0, 6.0, ((0, 128),)),
        "out_grad": centred(arg_keys[1], (TOKENS, D), 1.0, 6.0, ((0, 128),)),
        "gate_blocks": centred(arg_keys[2], (N_TENSOR * KB, BLK, BLK), (D // 2) ** -0.5, 0.125, ((0, 16),)),
        "up_blocks": centred(arg_keys[3], (N_TENSOR * KB, BLK, BLK), (D // 2) ** -0.5, 0.125, ((0, 16),)),
        "down_blocks": centred(arg_keys[4], (N_TENSOR * KB, BLK, BLK), (FF // 2) ** -0.5, 0.0625, ((0, 16),)),
        "gate_index": draw_gate_index(jax.random.fold_in(arg_keys[11], 71), 0),
        "up_index": draw_up_index(jax.random.fold_in(arg_keys[11], 71), 0),
        "down_index": draw_down_index(jax.random.fold_in(arg_keys[11], 71), 0),
        "gate_slot": draw_gate_slot(jax.random.fold_in(arg_keys[11], 71), 0),
        "up_slot": draw_up_slot(jax.random.fold_in(arg_keys[11], 71), 0),
        "down_slot": draw_down_slot(jax.random.fold_in(arg_keys[11], 71), 0),
    }


def rounded(value):
    return lax.optimization_barrier(value.astype(jnp.bfloat16)).astype(jnp.float32)

def col_sums(source, blocks, block_rows, block_cols, out_count):
    picked = jnp.take(source, block_rows, axis=1).astype(jnp.float32)
    product = jnp.einsum('tkd,kde->tke', picked, blocks.astype(jnp.float32), precision=lax.Precision.HIGHEST)
    onehot = (block_cols[:, None] == jnp.arange(out_count, dtype=jnp.int32)[None, :]).astype(jnp.float32)
    summed = jnp.einsum('tke,kc->tce', product, onehot, precision=lax.Precision.HIGHEST)
    return summed.reshape(summed.shape[0], out_count * blocks.shape[2])

def row_sums(source, blocks, block_rows, block_cols, out_count):
    picked = jnp.take(source, block_cols, axis=1).astype(jnp.float32)
    product = jnp.einsum('tke,kde->tkd', picked, blocks.astype(jnp.float32), precision=lax.Precision.HIGHEST)
    onehot = (block_rows[:, None] == jnp.arange(out_count, dtype=jnp.int32)[None, :]).astype(jnp.float32)
    summed = jnp.einsum('tkd,kr->trd', product, onehot, precision=lax.Precision.HIGHEST)
    return summed.reshape(summed.shape[0], out_count * blocks.shape[1])

def group_terms(left_side, right_side, block_rows, block_cols, factor):
    left_groups = left_side.reshape(N_DP, GROUP_TOK, left_side.shape[1], left_side.shape[2])
    right_groups = right_side.reshape(N_DP, GROUP_TOK, right_side.shape[1], right_side.shape[2])
    picked_left = jnp.take(left_groups, block_rows, axis=2).astype(jnp.float32)
    picked_right = jnp.take(right_groups, block_cols, axis=2).astype(jnp.float32)
    terms = jnp.einsum('gtkd,gtke->gkde', picked_left, picked_right, precision=lax.Precision.HIGHEST) * factor
    return lax.optimization_barrier(jnp.sum(rounded(terms), axis=0))

def reference(tokens, out_grad, gate_blocks, up_blocks, down_blocks, gate_index, up_index, down_index, gate_slot, up_slot, down_slot):
    ff_cols = FF_DEV // BLK
    d_cols = D // BLK
    token_blocks = tokens.reshape(TOKENS, d_cols, BLK)
    cot_blocks = out_grad.reshape(TOKENS, d_cols, BLK)
    factor = jnp.float32(1.0 / math.sqrt(TOKENS))

    def one_slice(carry, shard_id):
        out_acc, grad_acc = carry
        gate_part = lax.dynamic_slice_in_dim(gate_blocks, shard_id * KB, KB, 0)
        up_part = lax.dynamic_slice_in_dim(up_blocks, shard_id * KB, KB, 0)
        down_part = lax.dynamic_slice_in_dim(down_blocks, shard_id * KB, KB, 0)
        gate_ids = gate_index[shard_id]
        up_ids = up_index[shard_id]
        down_ids = down_index[shard_id]
        gate_rows, gate_cols = (gate_ids // ff_cols, gate_ids % ff_cols)
        up_rows, up_cols = (up_ids // ff_cols, up_ids % ff_cols)
        down_rows, down_cols = (down_ids // d_cols, down_ids % d_cols)
        gate_act = col_sums(token_blocks, gate_part, gate_rows, gate_cols, ff_cols)
        up_act = col_sums(token_blocks, up_part, up_rows, up_cols, ff_cols)
        sigma = jax.nn.sigmoid(gate_act)
        hidden = (gate_act * sigma * up_act).astype(jnp.bfloat16)
        hidden_blocks = hidden.reshape(TOKENS, ff_cols, BLK)
        down_partial = rounded(col_sums(hidden_blocks, down_part, down_rows, down_cols, d_cols))
        hidden_grad = row_sums(cot_blocks, down_part, down_rows, down_cols, ff_cols)
        gate_pre = (hidden_grad * up_act * sigma * (1.0 + gate_act * (1.0 - sigma))).astype(jnp.bfloat16)
        up_pre = (hidden_grad * gate_act * sigma).astype(jnp.bfloat16)
        gate_pre_blocks = gate_pre.reshape(TOKENS, ff_cols, BLK)
        up_pre_blocks = up_pre.reshape(TOKENS, ff_cols, BLK)
        input_partial = row_sums(gate_pre_blocks, gate_part, gate_rows, gate_cols, d_cols)
        input_partial = rounded(input_partial + row_sums(up_pre_blocks, up_part, up_rows, up_cols, d_cols))
        gate_sum = group_terms(token_blocks, gate_pre_blocks, gate_rows, gate_cols, factor)
        up_sum = group_terms(token_blocks, up_pre_blocks, up_rows, up_cols, factor)
        down_sum = group_terms(hidden_blocks, cot_blocks, down_rows, down_cols, factor)
        return ((out_acc + down_partial, grad_acc + input_partial), (gate_sum, up_sum, down_sum))
    start_acc = (jnp.zeros((TOKENS, D), jnp.float32), jnp.zeros((TOKENS, D), jnp.float32))
    (out_acc, grad_acc), (gate_all, up_all, down_all) = lax.scan(one_slice, start_acc, jnp.arange(N_TENSOR, dtype=jnp.int32))

    def place(slots, sums):
        return jnp.zeros((N_DP * CAP, BLK, BLK), jnp.float32).at[slots].set(sums)
    gate_grad = jax.vmap(place)(gate_slot, gate_all)
    up_grad = jax.vmap(place)(up_slot, up_all)
    down_grad = jax.vmap(place)(down_slot, down_all)
    return (out_acc.astype(jnp.bfloat16), grad_acc.astype(jnp.bfloat16), gate_grad, up_grad, down_grad)
```

```python
import functools
import math

import jax
import jax.numpy as jnp
from jax import lax
from jax.experimental import pallas as pl
from jax.experimental.pallas import tpu as pltpu
from jax.sharding import PartitionSpec as P

MESH = pl.DeviceIdType.MESH
D = 4096
BLK = 128
DC = 32
FC = 7
FDEV = 896
KB = 112
NBLK = 224
CAP = 17
TOK = 1024
F32 = jnp.float32
BF16 = jnp.bfloat16

THIRDS = ((0, 6, 11), (11, 17, 22), (22, 27, 32))
ORDERS = (("x", "y", "z"), ("y", "z", "x"), ("z", "x", "y"))


def kernel_body(
    tab,
    tok_ref,
    cot_ref,
    gb_ref,
    ub_ref,
    db_ref,
    lo_ref,
    tg_ref,
    gg_ref,
    ug_ref,
    dg_ref,
    buf,
    wgu,
    wd,
    stage,
    hid,
    gpre,
    part,
    got1,
    got2,
    mid,
    got3,
    ld_sem,
    ag_send,
    ag_recv,
    sib_send,
    sib_recv,
    rs_send,
    rs_recv,
):
    dp = lax.axis_index("dp")
    tp = lax.axis_index("tensor")
    ylo, z = dp // 4, dp % 4
    x, yhi, core = tp // 4, (tp // 2) % 2, tp % 2
    y = yhi * 2 + ylo
    here = {"x": x, "y": y, "z": z}

    def device(at, c):
        return (
            (at["y"] % 2) * 4 + at["z"],
            at["x"] * 4 + (at["y"] // 2) * 2 + c,
        )

    def moved(axis, step):
        at = dict(here)
        at[axis] = (here[axis] + step) % 4
        return at

    right = {a: device(moved(a, 1), core) for a in "xyz"}
    left = {a: device(moved(a, 3), core) for a in "xyz"}
    far = {a: device(moved(a, 2), core) for a in "xy"}
    sibling = device(here, 1 - core)

    barrier = pltpu.get_barrier_semaphore()
    partners = list(right.values()) + list(left.values()) + list(far.values()) + [sibling]
    for other in partners:
        pl.semaphore_signal(barrier, inc=1, device_id=other, device_id_type=MESH)
    pl.semaphore_wait(barrier, len(partners))

    def region(q, third, phase, along, lo, hi):
        axes = ORDERS[third]
        idx = []
        for a in ("z", "y", "x"):
            if a in axes[:phase]:
                idx.append(slice(None))
            elif a == axes[phase]:
                idx.append(along)
            else:
                idx.append(here[a])
        return buf.at[(q, pl.ds(lo, hi - lo), *idx, core)]

    def ag_copy(q, third, phase, k):
        lo, mid_col, hi = THIRDS[third]
        axis = ORDERS[third][phase]
        own = here[axis]
        along, cols, to = (
            (own, (lo, mid_col), right),
            (own, (mid_col, hi), left),
            (own, (mid_col, hi), right),
            (own, (lo, mid_col), left),
            ((own + 3) % 4, (lo, mid_col), right),
            ((own + 1) % 4, (mid_col, hi), left),
        )[k]
        ref = region(q, third, phase, along, *cols)
        return pltpu.make_async_remote_copy(
            src_ref=ref,
            dst_ref=ref,
            send_sem=ag_send.at[q, third, phase, k],
            recv_sem=ag_recv.at[q, third, phase, k],
            device_id=to[axis],
            device_id_type=MESH,
        )

    def sib_copy(q, third, k):
        lo, _, hi = THIRDS[third]
        axis = ORDERS[third][2]
        ref = region(q, third, 2, (here[axis] + k) % 4, lo, hi)
        return pltpu.make_async_remote_copy(
            src_ref=ref,
            dst_ref=ref,
            send_sem=sib_send.at[q, third, k],
            recv_sem=sib_recv.at[q, third, k],
            device_id=sibling,
            device_id_type=MESH,
        )

    def ag_start(q, phase):
        for k in range(4):
            for third in range(3):
                ag_copy(q, third, phase, k).start()

    def ag_forward(q, phase):
        for third in range(3):
            ag_copy(q, third, phase, 0).wait_recv()
            ag_copy(q, third, phase, 4).start()
            ag_copy(q, third, phase, 1).wait_recv()
            ag_copy(q, third, phase, 5).start()

    def ag_direct(q, phase):
        for third in range(3):
            ag_copy(q, third, phase, 2).wait_recv()
            ag_copy(q, third, phase, 3).wait_recv()

    def ag_far(q, phase):
        for third in range(3):
            ag_copy(q, third, phase, 4).wait_recv()
            ag_copy(q, third, phase, 5).wait_recv()

    def sib_start(q, k):
        for third in range(3):
            sib_copy(q, third, k).start()

    def sib_wait(q):
        for third in range(3):
            for k in range(4):
                sib_copy(q, third, k).wait_recv()

    def ag_finish(q):
        for third in range(3):
            for phase in range(3):
                for k in range(6):
                    ag_copy(q, third, phase, k).wait_send()
            for k in range(4):
                sib_copy(q, third, k).wait_send()

    def load(src):
        return pltpu.make_async_copy(src, stage.at[pl.ds(0, KB)], ld_sem)

    def spread_cols(base, side):
        @pl.loop(0, DC)
        def _(r):
            for c in range(FC):
                rows = pl.ds(pl.multiple_of(r * BLK, BLK), BLK)
                wgu[rows, pl.ds((2 * c + side) * BLK, BLK)] = stage[tab[base + r * FC + c]]

    def spread_rows(base):
        @pl.loop(0, FC)
        def _(r):
            for c in range(DC):
                rows = pl.ds(pl.multiple_of(r * BLK, BLK), BLK)
                wd[rows, pl.ds(c * BLK, BLK)] = stage[tab[base + r * DC + c]]

    for j in range(DC):
        cols = pl.ds(j * BLK, BLK)
        buf[0, j, z, y, x, core] = tok_ref[:, cols]
        buf[1, j, z, y, x, core] = cot_ref[:, cols]
    ag_start(0, 0)
    ag_start(1, 0)
    load(gb_ref).start()
    stage[KB] = jnp.zeros((BLK, BLK), BF16)
    ag_forward(0, 0)
    ag_direct(0, 0)
    ag_far(0, 0)
    ag_start(0, 1)
    ag_forward(1, 0)
    ag_direct(1, 0)
    ag_far(1, 0)
    ag_start(1, 1)
    ag_forward(0, 1)
    ag_direct(0, 1)
    ag_far(0, 1)
    ag_start(0, 2)
    sib_start(0, 0)
    ag_forward(1, 1)
    ag_direct(1, 1)
    ag_far(1, 1)
    load(gb_ref).wait()
    spread_cols(0, 0)
    load(ub_ref).start()
    ag_forward(0, 2)
    ag_start(1, 2)
    sib_start(1, 0)
    load(ub_ref).wait()
    spread_cols(NBLK, 1)
    load(db_ref).start()
    ag_direct(0, 2)
    sib_start(0, 1)
    sib_start(0, 3)
    load(db_ref).wait()
    spread_rows(2 * NBLK)
    ag_far(0, 2)
    sib_start(0, 2)
    sib_wait(0)

    flat = buf.reshape(2, DC, TOK, BLK)
    MT = 256

    def rows_of(q, rows):
        return jnp.concatenate([flat[q, j, rows, :] for j in range(DC)], axis=1)

    def forward_cols(c):
        @pl.loop(0, TOK // MT)
        def _(m):
            rows = pl.ds(pl.multiple_of(m * MT, MT), MT)
            both = jnp.dot(
                rows_of(0, rows), wgu[:, pl.ds(c * 2 * BLK, 2 * BLK)], preferred_element_type=F32
            )
            gate, up = both[:, :BLK], both[:, BLK:]
            sigma = 1.0 / (1.0 + jnp.exp(-gate))
            swish = gate * sigma
            hid[c, rows, :] = (swish * up).astype(BF16)
            gpre[2 * c, rows, :] = (
                up * sigma * (1.0 + gate * (1.0 - sigma))
            ).astype(BF16)
            gpre[2 * c + 1, rows, :] = swish.astype(BF16)

    forward_cols(0)
    ag_forward(1, 2)
    forward_cols(1)
    ag_direct(1, 2)
    sib_start(1, 1)
    sib_start(1, 3)
    for c in range(2, FC):
        forward_cols(c)
    ag_far(1, 2)
    sib_start(1, 2)

    def own_rows(ref):
        runs = []
        for h in range(2):
            rows = pl.ds(pl.multiple_of((z * 4 + h * 2 + ylo) * 64, 64), 64)
            runs.append(jnp.concatenate([ref[j, rows, :] for j in range(ref.shape[0])], axis=1))
        return jnp.concatenate(runs, axis=0)

    def partial_out(o, left_side, weights, contract):
        width = 512

        @pl.loop(0, D // width)
        def _(n):
            cols = pl.ds(pl.multiple_of(n * width, width), width)
            w = weights[:, cols] if contract == 0 else weights[cols, :]
            term = lax.dot_general(
                left_side, w, (((1,), (contract,)), ((), ())), preferred_element_type=F32
            ).astype(BF16)
            part[o, :, :, :, :, cols] = term.reshape(2, 4, 2, 8, width)

    def rs_copy(o, k):
        if k == 0:
            src, dst, to = part.at[o, :, :, 1 - core], got1.at[o], sibling
        elif k < 4:
            at = moved("x", k)
            src, dst, to = part.at[o, :, at["x"], core], got2.at[o, k - 1], device(at, core)
        else:
            src, dst, to = mid.at[o, 1 - yhi], got3.at[o], far["y"]
        return pltpu.make_async_remote_copy(
            src_ref=src,
            dst_ref=dst,
            send_sem=rs_send.at[o, k],
            recv_sem=rs_recv.at[o, k],
            device_id=to,
            device_id_type=MESH,
        )

    def rs_one(o):
        rs_copy(o, 0).start()

    def rs_two(o):
        rs_copy(o, 0).wait_recv()
        for h in range(2):
            for w in range(4):
                part[o, h, w, core] = (
                    part[o, h, w, core].astype(F32) + got1[o, h, w].astype(F32)
                ).astype(BF16)
        for k in (2, 1, 3):
            rs_copy(o, k).start()

    def rs_three(o):
        for k in range(1, 4):
            rs_copy(o, k).wait_recv()
        for h in range(2):
            total = part[o, h, x, core].astype(F32)
            for k in range(3):
                total = total + got2[o, k, h].astype(F32)
            mid[o, h] = total.astype(BF16)
        rs_copy(o, 4).start()

    def rs_four(o, out):
        rs_copy(o, 4).wait_recv()
        out[...] = (mid[o, yhi].astype(F32) + got3[o].astype(F32)).astype(BF16)
        for k in range(5):
            rs_copy(o, k).wait_send()

    partial_out(0, own_rows(hid), wd, 0)
    rs_one(0)
    sib_wait(1)

    def backward_cols(start, width):
        @pl.loop(0, TOK // MT)
        def _(m):
            rows = pl.ds(pl.multiple_of(m * MT, MT), MT)
            grad = lax.dot_general(
                rows_of(1, rows),
                wd[pl.ds(start * BLK, width * BLK), :],
                (((1,), (1,)), ((), ())),
                preferred_element_type=F32,
            )
            for j in range(width):
                piece = grad[:, j * BLK : (j + 1) * BLK]
                for side in range(2):
                    k = 2 * (start + j) + side
                    gpre[k, rows, :] = (gpre[k, rows, :].astype(F32) * piece).astype(BF16)

    backward_cols(0, 2)
    rs_two(0)
    backward_cols(2, 2)
    backward_cols(4, 2)
    rs_three(0)
    backward_cols(6, 1)
    partial_out(1, own_rows(gpre), wgu, 1)
    rs_one(1)

    factor = 1.0 / math.sqrt(TOK)

    def grads(base, left, right, out):
        @pl.loop(0, CAP)
        def _(v):
            weight = tab[base + 2 * CAP + v].astype(F32) * factor
            a = left(tab[base + v])
            b = right(tab[base + CAP + v])
            out[v] = (
                lax.dot_general(a, b, (((0,), (0,)), ((), ())), preferred_element_type=F32) * weight
            )

    def token_block(row):
        return buf[0, row].reshape(TOK, BLK)

    def cot_block(col):
        return buf[1, col].reshape(TOK, BLK)

    slots = 3 * NBLK
    rs_two(1)
    grads(slots, token_block, lambda col: gpre[2 * col], gg_ref)
    rs_three(1)
    rs_four(0, lo_ref)
    grads(slots + 3 * CAP, token_block, lambda col: gpre[2 * col + 1], ug_ref)
    rs_four(1, tg_ref)
    grads(slots + 6 * CAP, lambda row: hid[row], cot_block, dg_ref)
    ag_finish(0)
    ag_finish(1)


def tables(ids, slots, cols, me):
    match = ids[None, :] == jnp.arange(NBLK, dtype=jnp.int32)[:, None]
    order = jnp.arange(KB, dtype=jnp.int32)[None, :]
    where = KB + jnp.sum(jnp.where(match, order - KB, 0), axis=1)
    mine = slots[None, :] == me * CAP + jnp.arange(CAP, dtype=jnp.int32)[:, None]
    row = jnp.sum(jnp.where(mine, ids[None, :] // cols, 0), axis=1)
    col = jnp.sum(jnp.where(mine, ids[None, :] % cols, 0), axis=1)
    full = jnp.sum(mine.astype(jnp.int32), axis=1)
    return where, jnp.concatenate([row, col, full])


def local(
    tokens,
    out_grad,
    gate_blocks,
    up_blocks,
    down_blocks,
    gate_index,
    up_index,
    down_index,
    gate_slot,
    up_slot,
    down_slot,
):
    me = lax.axis_index("dp")
    parts = [
        tables(gate_index[0], gate_slot[0], FC, me),
        tables(up_index[0], up_slot[0], FC, me),
        tables(down_index[0], down_slot[0], DC, me),
    ]
    tab = jnp.concatenate([p[0] for p in parts] + [p[1] for p in parts])
    vmem = pl.BlockSpec(memory_space=pltpu.VMEM)
    hbm = pl.BlockSpec(memory_space=pl.ANY)
    rows = jax.ShapeDtypeStruct((8, D), BF16)
    owned = jax.ShapeDtypeStruct((CAP, BLK, BLK), F32)
    lo, tg, gg, ug, dg = pl.pallas_call(
        kernel_body,
        out_shape=(rows, rows, owned, owned, owned),
        in_specs=[pl.BlockSpec(memory_space=pltpu.SMEM), vmem, vmem, hbm, hbm, hbm],
        out_specs=(vmem,) * 5,
        scratch_shapes=[
            pltpu.VMEM((2, DC, 4, 4, 4, 2, 8, BLK), BF16),
            pltpu.VMEM((D, 2 * FDEV), BF16),
            pltpu.VMEM((FDEV, D), BF16),
            pltpu.VMEM((KB + 1, BLK, BLK), BF16),
            pltpu.VMEM((FC, TOK, BLK), BF16),
            pltpu.VMEM((2 * FC, TOK, BLK), BF16),
            pltpu.VMEM((2, 2, 4, 2, 8, D), BF16),
            pltpu.VMEM((2, 2, 4, 8, D), BF16),
            pltpu.VMEM((2, 3, 2, 8, D), BF16),
            pltpu.VMEM((2, 2, 8, D), BF16),
            pltpu.VMEM((2, 8, D), BF16),
            pltpu.SemaphoreType.DMA,
            pltpu.SemaphoreType.DMA((2, 3, 3, 6)),
            pltpu.SemaphoreType.DMA((2, 3, 3, 6)),
            pltpu.SemaphoreType.DMA((2, 3, 4)),
            pltpu.SemaphoreType.DMA((2, 3, 4)),
            pltpu.SemaphoreType.DMA((2, 5)),
            pltpu.SemaphoreType.DMA((2, 5)),
        ],
        compiler_params=pltpu.CompilerParams(
            collective_id=0, has_side_effects=True, vmem_limit_bytes=61 * 1024 * 1024
        ),
    )(tab, tokens, out_grad, gate_blocks, up_blocks, down_blocks)
    return lo, tg, gg[None], ug[None], dg[None]


def solution(mesh):
    in_specs = (
        P(("dp", "tensor"), None),
        P(("dp", "tensor"), None),
        P("tensor", None, None),
        P("tensor", None, None),
        P("tensor", None, None),
        P("tensor", None),
        P("tensor", None),
        P("tensor", None),
        P("tensor", None),
        P("tensor", None),
        P("tensor", None),
    )
    out_specs = (
        P(("dp", "tensor"), None),
        P(("dp", "tensor"), None),
        P("tensor", "dp", None, None),
        P("tensor", "dp", None, None),
        P("tensor", "dp", None, None),
    )
    return jax.shard_map(local, mesh=mesh, in_specs=in_specs, out_specs=out_specs, check_vma=False)
```

```python
import functools
import math

import jax
import jax.numpy as jnp
from jax import lax
from jax.experimental import pallas as pl
from jax.experimental.pallas import tpu as pltpu
from jax.sharding import PartitionSpec as P

MESH = pl.DeviceIdType.MESH
D = 4096
BLK = 128
DC = 32
FC = 7
FDEV = 896
KB = 112
NBLK = 224
CAP = 17
TOK = 1024
F32 = jnp.float32
BF16 = jnp.bfloat16

THIRDS = ((0, 6, 12), (12, 17, 22), (22, 27, 32))
ORDERS = (("x", "y", "z"), ("y", "z", "x"), ("z", "x", "y"))


def kernel_body(
    tok_ref,
    cot_ref,
    gb_ref,
    ub_ref,
    db_ref,
    gi_ref,
    ui_ref,
    di_ref,
    gs_ref,
    us_ref,
    ds_ref,
    lo_ref,
    tg_ref,
    gg_ref,
    ug_ref,
    dg_ref,
    gi,
    ui,
    di,
    giv,
    uiv,
    div,
    gsv,
    usv,
    dsv,
    picks,
    taken,
    where,
    buf,
    wgu,
    wd,
    stage,
    acc,
    hid,
    gpre,
    part,
    got1,
    got2,
    mid,
    got3,
    rows_out,
    grad_out,
    in_sem,
    ld_sem,
    out_sem,
    ag_send,
    ag_recv,
    sib_send,
    sib_recv,
    rs_send,
    rs_recv,
):
    dp = lax.axis_index("dp")
    tp = lax.axis_index("tensor")
    ylo, z = dp // 4, dp % 4
    x, yhi, core = tp // 4, (tp // 2) % 2, tp % 2
    y = yhi * 2 + ylo
    here = {"x": x, "y": y, "z": z}

    def device(at, c):
        return (
            (at["y"] % 2) * 4 + at["z"],
            at["x"] * 4 + (at["y"] // 2) * 2 + c,
        )

    def moved(axis, step):
        at = dict(here)
        at[axis] = (here[axis] + step) % 4
        return at

    right = {a: device(moved(a, 1), core) for a in "xyz"}
    left = {a: device(moved(a, 3), core) for a in "xyz"}
    far = {a: device(moved(a, 2), core) for a in "xyz"}
    sibling = device(here, 1 - core)

    small = [
        pltpu.make_async_copy(src, dst, in_sem.at[n])
        for n, (src, dst) in enumerate(
            (
                (gi_ref, gi),
                (ui_ref, ui),
                (di_ref, di),
                (gi_ref, giv),
                (ui_ref, uiv),
                (di_ref, div),
                (gs_ref, gsv),
                (us_ref, usv),
                (ds_ref, dsv),
            )
        )
    ]

    def load(src):
        return pltpu.make_async_copy(src, stage.at[pl.ds(0, KB)], ld_sem)

    barrier = pltpu.get_barrier_semaphore()
    partners = list(right.values()) + list(left.values()) + list(far.values()) + [sibling]
    for other in partners:
        pl.semaphore_signal(barrier, inc=1, device_id=other, device_id_type=MESH)
    for copy in small:
        copy.start()
    load(gb_ref).start()
    for j in range(DC):
        cols = pl.ds(j * BLK, BLK)
        buf[0, j, z, y, x, core] = tok_ref[:, cols]
        buf[1, j, z, y, x, core] = cot_ref[:, cols]
    pl.semaphore_wait(barrier, len(partners))

    def plane(axis, along):
        return tuple(along if a == axis else slice(None) for a in ("z", "y", "x"))

    def region(q, third, phase, along, lo, hi):
        axes = ORDERS[third]
        idx = []
        for a in ("z", "y", "x"):
            if a in axes[:phase]:
                idx.append(slice(None))
            elif a == axes[phase]:
                idx.append(along)
            else:
                idx.append(here[a])
        return buf.at[(q, pl.ds(lo, hi - lo), *idx, core)]

    def ag_copy(q, third, phase, k):
        lo, mid_col, hi = THIRDS[third]
        axis = ORDERS[third][phase]
        own = here[axis]
        if phase == 0:
            along, cols, to = own, (lo, hi), (right, left, far)[k]
        else:
            along, cols, to = (
                (own, (lo, mid_col), right),
                (own, (mid_col, hi), left),
                (own, (mid_col, hi), right),
                (own, (lo, mid_col), left),
                ((own + 3) % 4, (lo, mid_col), right),
                ((own + 1) % 4, (mid_col, hi), left),
            )[k]
        ref = region(q, third, phase, along, *cols)
        return pltpu.make_async_remote_copy(
            src_ref=ref,
            dst_ref=ref,
            send_sem=ag_send.at[q, third, phase, k],
            recv_sem=ag_recv.at[q, third, phase, k],
            device_id=to[axis],
            device_id_type=MESH,
        )

    def sib_copy(q, third, k):
        lo, _, hi = THIRDS[third]
        axis = ORDERS[third][2]
        ref = region(q, third, 2, (here[axis] + k) % 4, lo, hi)
        return pltpu.make_async_remote_copy(
            src_ref=ref,
            dst_ref=ref,
            send_sem=sib_send.at[q, third, k],
            recv_sem=sib_recv.at[q, third, k],
            device_id=sibling,
            device_id_type=MESH,
        )

    def ag_start(q, phase):
        for k in range(4 if phase else 3):
            for third in range(3):
                ag_copy(q, third, phase, k).start()

    def ag_line(q):
        for third in range(3):
            for k in range(3):
                ag_copy(q, third, 0, k).wait_recv()

    def ag_forward(q, phase):
        for third in range(3):
            ag_copy(q, third, phase, 0).wait_recv()
            ag_copy(q, third, phase, 4).start()
            ag_copy(q, third, phase, 1).wait_recv()
            ag_copy(q, third, phase, 5).start()

    def ag_direct(q, phase):
        for third in range(3):
            ag_copy(q, third, phase, 2).wait_recv()
            ag_copy(q, third, phase, 3).wait_recv()

    def ag_far(q, phase):
        for third in range(3):
            ag_copy(q, third, phase, 4).wait_recv()
            ag_copy(q, third, phase, 5).wait_recv()

    def sib_start(q, k):
        for third in range(3):
            sib_copy(q, third, k).start()

    def sib_wait(q, third, k):
        sib_copy(q, third, k).wait_recv()

    def ag_finish(q):
        for third in range(3):
            for k in range(3):
                ag_copy(q, third, 0, k).wait_send()
            for phase in (1, 2):
                for k in range(6):
                    ag_copy(q, third, phase, k).wait_send()
            for k in range(4):
                sib_copy(q, third, k).wait_send()

    def find_blocks():
        for n in range(3):
            taken[n] = 0

        @pl.loop(0, DC)
        def _(r):
            for c in range(FC):
                number = r * FC + c
                for n, ids in enumerate((gi, ui, di)):
                    at = jnp.minimum(taken[n], KB - 1)
                    hit = ids[0, at] == number
                    where[n, number] = jnp.where(hit, at, KB)
                    taken[n] = taken[n] + hit.astype(jnp.int32)

    def spread(n, per, store, lo, hi):
        @pl.loop(lo, hi)
        def _(r):
            for c in range(per):
                store(r, c, stage[where[n, r * per + c]])

    def block_rows(r):
        return pl.ds(pl.multiple_of(r * BLK, BLK), BLK)

    def store_gate(r, c, block):
        wgu[c, block_rows(r), pl.ds(0, BLK)] = block

    def store_up(r, c, block):
        wgu[c, block_rows(r), pl.ds(BLK, BLK)] = block

    def store_down(r, c, block):
        wd[block_rows(r), pl.ds(c * BLK, BLK)] = block

    def rows_at(q, third, ks):
        lo, _, hi = THIRDS[third]
        axis = ORDERS[third][2]
        runs = []
        for k in ks:
            at = plane(axis, (here[axis] + k) % 4)
            runs.append(
                jnp.concatenate(
                    [buf[(q, j, *at)].reshape(256, BLK) for j in range(lo, hi)], axis=1
                )
            )
        return jnp.concatenate(runs, axis=0)

    def add_to(n, third, ks, term):
        axis = ORDERS[third][2]
        for s, k in enumerate(ks):
            at = (n, *plane(axis, (here[axis] + k) % 4))
            acc[at] = acc[at] + term[s * 256 : (s + 1) * 256].reshape(4, 4, 16, BLK)

    def forward_step(third, ks):
        lo, _, hi = THIRDS[third]
        for k in ks:
            sib_wait(0, third, k)

        @pl.loop(0, FC)
        def _(c):
            both = jnp.dot(
                rows_at(0, third, ks),
                wgu[c, pl.ds(lo * BLK, (hi - lo) * BLK), :],
                preferred_element_type=F32,
            )
            add_to(2 * c, third, ks, both[:, :BLK])
            add_to(2 * c + 1, third, ks, both[:, BLK:])

    def backward_step(third, ks):
        lo, _, hi = THIRDS[third]
        for k in ks:
            sib_wait(1, third, k)

        def some(start, width):
            grad = lax.dot_general(
                rows_at(1, third, ks),
                wd[pl.ds(start * BLK, width * BLK), pl.ds(lo * BLK, (hi - lo) * BLK)],
                (((1,), (1,)), ((), ())),
                preferred_element_type=F32,
            )
            for j in range(width):
                add_to(start + j, third, ks, grad[:, j * BLK : (j + 1) * BLK])

        @pl.loop(0, 3)
        def _(c):
            some(2 * c, 2)

        some(6, 1)

    def point_forward():
        @pl.loop(0, FC)
        def _(c):
            @pl.loop(0, 4)
            def _(m):
                rows = pl.ds(pl.multiple_of(m * 256, 256), 256)
                gate = acc[2 * c, m].reshape(256, BLK)
                up = acc[2 * c + 1, m].reshape(256, BLK)
                sigma = 1.0 / (1.0 + jnp.exp(-gate))
                swish = gate * sigma
                hid[c, rows, :] = (swish * up).astype(BF16)
                gpre[2 * c, rows, :] = (up * sigma * (1.0 + gate * (1.0 - sigma))).astype(BF16)
                gpre[2 * c + 1, rows, :] = swish.astype(BF16)
                acc[2 * c, m] = jnp.zeros((4, 4, 16, BLK), F32)
                acc[2 * c + 1, m] = jnp.zeros((4, 4, 16, BLK), F32)

    def point_backward():
        @pl.loop(0, FC)
        def _(c):
            @pl.loop(0, 4)
            def _(m):
                rows = pl.ds(pl.multiple_of(m * 256, 256), 256)
                grad = acc[c, m].reshape(256, BLK)
                for side in range(2):
                    gpre[2 * c + side, rows, :] = (
                        gpre[2 * c + side, rows, :].astype(F32) * grad
                    ).astype(BF16)

    def own_rows(ref):
        runs = []
        for h in range(2):
            rows = pl.ds(pl.multiple_of((z * 4 + h * 2 + ylo) * 64, 64), 64)
            runs.append(jnp.concatenate([ref[j, rows, :] for j in range(ref.shape[0])], axis=1))
        return jnp.concatenate(runs, axis=0)

    def partial_out(o):
        width = 512

        @pl.loop(0, D // width)
        def _(n):
            cols = pl.ds(pl.multiple_of(n * width, width), width)
            if o == 0:
                term = jnp.dot(own_rows(hid), wd[:, cols], preferred_element_type=F32)
            else:
                term = lax.dot_general(
                    own_rows(gpre),
                    jnp.concatenate([wgu[c, cols, :] for c in range(FC)], axis=1),
                    (((1,), (1,)), ((), ())),
                    preferred_element_type=F32,
                )
            part[o, :, :, :, :, cols] = term.astype(BF16).reshape(2, 4, 2, 8, width)

    def rs_copy(o, k):
        if k == 0:
            src, dst, to = part.at[o, :, :, 1 - core], got1.at[o], sibling
        elif k < 4:
            at = moved("x", k)
            src, dst, to = part.at[o, :, at["x"], core], got2.at[o, k - 1], device(at, core)
        else:
            src, dst, to = mid.at[o, 1 - yhi], got3.at[o], far["y"]
        return pltpu.make_async_remote_copy(
            src_ref=src,
            dst_ref=dst,
            send_sem=rs_send.at[o, k],
            recv_sem=rs_recv.at[o, k],
            device_id=to,
            device_id_type=MESH,
        )

    def rs_one(o):
        rs_copy(o, 0).start()

    def rs_two(o):
        rs_copy(o, 0).wait_recv()
        for h in range(2):
            for w in range(4):
                part[o, h, w, core] = (
                    part[o, h, w, core].astype(F32) + got1[o, h, w].astype(F32)
                ).astype(BF16)
        for k in (2, 1, 3):
            rs_copy(o, k).start()

    def rs_three(o):
        for k in range(1, 4):
            rs_copy(o, k).wait_recv()
        for h in range(2):
            total = part[o, h, x, core].astype(F32)
            for k in range(3):
                total = total + got2[o, k, h].astype(F32)
            mid[o, h] = total.astype(BF16)
        rs_copy(o, 4).start()

    def row_copy(o):
        return pltpu.make_async_copy(rows_out.at[o], (lo_ref, tg_ref)[o], out_sem.at[o])

    def rs_four(o):
        rs_copy(o, 4).wait_recv()
        rows_out[o] = (mid[o, yhi].astype(F32) + got3[o].astype(F32)).astype(BF16)
        row_copy(o).start()
        for k in range(5):
            rs_copy(o, k).wait_send()

    def pick_slots():
        @pl.loop(0, CAP)
        def _(v):
            mine = dp * CAP + v
            for n, (ids, slots) in enumerate(((giv, gsv), (uiv, usv), (div, dsv))):
                picks[n, v] = jnp.sum(jnp.where(slots[...] == mine, ids[...] + 1, 0))

    factor = 1.0 / math.sqrt(TOK)

    def block_grad(left, right, weight):
        return (
            lax.dot_general(left, right, (((0,), (0,)), ((), ())), preferred_element_type=F32)
            * weight
        )

    def grads(lo, hi):
        @pl.loop(lo, hi)
        def _(v):
            for n in range(3):
                number = picks[n, v]
                block = jnp.maximum(number - 1, 0)
                weight = jnp.where(number > 0, factor, 0.0)
                if n < 2:
                    left = buf[0, block // FC].reshape(TOK, BLK)
                    right = gpre[2 * (block % FC) + n]
                else:
                    left = hid[block // DC]
                    right = buf[1, block % DC].reshape(TOK, BLK)
                grad_out[n, v] = block_grad(left, right, weight)

    def grad_copy(n):
        return pltpu.make_async_copy(grad_out.at[n], (gg_ref, ug_ref, dg_ref)[n], out_sem.at[2 + n])

    ag_start(0, 0)
    ag_start(1, 0)
    stage[KB] = jnp.zeros((BLK, BLK), BF16)
    for copy in small:
        copy.wait()

    @pl.loop(0, 2 * FC)
    def _(n):
        acc[n] = jnp.zeros((4, 4, 4, 16, BLK), F32)

    find_blocks()
    ag_line(0)
    ag_start(0, 1)
    load(gb_ref).wait()
    spread(0, FC, store_gate, 0, 8)
    ag_line(1)
    ag_start(1, 1)
    spread(0, FC, store_gate, 8, 16)
    ag_forward(0, 1)
    spread(0, FC, store_gate, 16, DC)
    load(ub_ref).start()
    ag_direct(0, 1)
    ag_far(0, 1)
    ag_start(0, 2)
    sib_start(0, 0)
    ag_forward(1, 1)
    load(ub_ref).wait()
    spread(1, FC, store_up, 0, 16)
    ag_direct(1, 1)
    ag_far(1, 1)
    sib_start(1, 0)
    spread(1, FC, store_up, 16, DC)
    load(db_ref).start()
    forward_step(0, (0,))
    ag_forward(0, 2)
    forward_step(1, (0,))
    forward_step(2, (0,))
    load(db_ref).wait()
    spread(2, DC, store_down, 0, FC)
    ag_direct(0, 2)
    ag_start(1, 2)
    sib_start(0, 1)
    sib_start(0, 3)
    pick_slots()
    forward_step(0, (1, 3))
    ag_far(0, 2)
    sib_start(0, 2)
    forward_step(1, (1, 3))
    ag_forward(1, 2)
    forward_step(2, (1, 3))
    for third in range(3):
        forward_step(third, (2,))
    point_forward()
    ag_direct(1, 2)
    sib_start(1, 1)
    sib_start(1, 3)
    partial_out(0)
    rs_one(0)
    for third in range(3):
        backward_step(third, (0,))
    rs_two(0)
    ag_far(1, 2)
    sib_start(1, 2)
    for third in range(3):
        backward_step(third, (1, 3))
    rs_three(0)
    for third in range(3):
        backward_step(third, (2,))
    point_backward()
    partial_out(1)
    rs_one(1)
    grads(0, 3)
    rs_two(1)
    rs_four(0)
    grads(3, 9)
    rs_three(1)
    grads(9, 13)
    rs_four(1)
    grads(13, CAP)
    for n in range(3):
        grad_copy(n).start()
    ag_finish(0)
    ag_finish(1)
    for o in range(2):
        row_copy(o).wait()
    for n in range(3):
        grad_copy(n).wait()


def copy_body(*refs):
    sources, targets, sem = refs[:5], refs[5:10], refs[10]
    copies = [pltpu.make_async_copy(a, b, sem.at[n]) for n, (a, b) in enumerate(zip(sources, targets))]
    for copy in copies:
        copy.start()
    for copy in copies:
        copy.wait()


def local(
    tokens,
    out_grad,
    gate_blocks,
    up_blocks,
    down_blocks,
    gate_index,
    up_index,
    down_index,
    gate_slot,
    up_slot,
    down_slot,
):
    hbm = pl.BlockSpec(memory_space=pl.ANY)
    vmem = pl.BlockSpec(memory_space=pltpu.VMEM)
    rows = jax.ShapeDtypeStruct((8, D), BF16)
    owned = jax.ShapeDtypeStruct((CAP, BLK, BLK), F32)
    shapes = (rows, rows, owned, owned, owned)
    results = pl.pallas_call(
        kernel_body,
        out_shape=shapes,
        in_specs=[vmem, vmem] + [hbm] * 9,
        out_specs=(hbm,) * 5,
        scratch_shapes=[pltpu.SMEM((1, KB), jnp.int32)] * 3
        + [pltpu.VMEM((1, KB), jnp.int32)] * 6
        + [
            pltpu.SMEM((3, CAP), jnp.int32),
            pltpu.SMEM((3,), jnp.int32),
            pltpu.SMEM((3, NBLK), jnp.int32),
            pltpu.VMEM((2, DC, 4, 4, 4, 2, 8, BLK), BF16),
            pltpu.VMEM((FC, D, 2 * BLK), BF16),
            pltpu.VMEM((FDEV, D), BF16),
            pltpu.VMEM((KB + 1, BLK, BLK), BF16),
            pltpu.VMEM((2 * FC, 4, 4, 4, 16, BLK), F32),
            pltpu.VMEM((FC, TOK, BLK), BF16),
            pltpu.VMEM((2 * FC, TOK, BLK), BF16),
            pltpu.VMEM((2, 2, 4, 2, 8, D), BF16),
            pltpu.VMEM((2, 2, 4, 8, D), BF16),
            pltpu.VMEM((2, 3, 2, 8, D), BF16),
            pltpu.VMEM((2, 2, 8, D), BF16),
            pltpu.VMEM((2, 8, D), BF16),
            pltpu.VMEM((2, 8, D), BF16),
            pltpu.VMEM((3, CAP, BLK, BLK), F32),
            pltpu.SemaphoreType.DMA((9,)),
            pltpu.SemaphoreType.DMA,
            pltpu.SemaphoreType.DMA((5,)),
            pltpu.SemaphoreType.DMA((2, 3, 3, 6)),
            pltpu.SemaphoreType.DMA((2, 3, 3, 6)),
            pltpu.SemaphoreType.DMA((2, 3, 4)),
            pltpu.SemaphoreType.DMA((2, 3, 4)),
            pltpu.SemaphoreType.DMA((2, 5)),
            pltpu.SemaphoreType.DMA((2, 5)),
        ],
        compiler_params=pltpu.CompilerParams(
            collective_id=0, has_side_effects=True, vmem_limit_bytes=62 * 1024 * 1024
        ),
    )(
        tokens,
        out_grad,
        gate_blocks,
        up_blocks,
        down_blocks,
        gate_index,
        up_index,
        down_index,
        gate_slot,
        up_slot,
        down_slot,
    )
    lo, tg, gg, ug, dg = pl.pallas_call(
        copy_body,
        out_shape=shapes,
        in_specs=[hbm] * 5,
        out_specs=(hbm,) * 5,
        scratch_shapes=[pltpu.SemaphoreType.DMA((5,))],
    )(*results)
    return lo, tg, gg[None], ug[None], dg[None]


def solution(mesh):
    in_specs = (
        P(("dp", "tensor"), None),
        P(("dp", "tensor"), None),
        P("tensor", None, None),
        P("tensor", None, None),
        P("tensor", None, None),
        P("tensor", None),
        P("tensor", None),
        P("tensor", None),
        P("tensor", None),
        P("tensor", None),
        P("tensor", None),
    )
    out_specs = (
        P(("dp", "tensor"), None),
        P(("dp", "tensor"), None),
        P("tensor", "dp", None, None),
        P("tensor", "dp", None, None),
        P("tensor", "dp", None, None),
    )
    return jax.shard_map(local, mesh=mesh, in_specs=in_specs, out_specs=out_specs, check_vma=False)
```

```python
import functools
import math

import jax
import jax.numpy as jnp
from jax import lax
from jax.experimental import pallas as pl
from jax.experimental.pallas import tpu as pltpu
from jax.sharding import PartitionSpec as P

MESH = pl.DeviceIdType.MESH
D = 4096
BLK = 128
DC = 32
FC = 7
FDEV = 896
KB = 112
NBLK = 224
CAP = 17
TOK = 1024
F32 = jnp.float32
BF16 = jnp.bfloat16

THIRDS = ((0, 6, 12), (12, 17, 22), (22, 27, 32))
ORDERS = (("x", "y", "z"), ("y", "z", "x"), ("z", "x", "y"))


def kernel_body(
    tok_ref,
    cot_ref,
    gb_ref,
    ub_ref,
    db_ref,
    gi_ref,
    ui_ref,
    di_ref,
    gs_ref,
    us_ref,
    ds_ref,
    lo_ref,
    tg_ref,
    gg_ref,
    ug_ref,
    dg_ref,
    gi,
    ui,
    di,
    giv,
    uiv,
    div,
    gsv,
    usv,
    dsv,
    picks,
    taken,
    where,
    buf,
    wgu,
    wd,
    stage,
    hid,
    gpre,
    own_g,
    part,
    got1,
    got2,
    mid,
    got3,
    rows_out,
    grad_out,
    in_sem,
    ld_sem,
    out_sem,
    ag_send,
    ag_recv,
    sib_send,
    sib_recv,
    rs_send,
    rs_recv,
):
    dp = lax.axis_index("dp")
    tp = lax.axis_index("tensor")
    ylo, z = dp // 4, dp % 4
    x, yhi, core = tp // 4, (tp // 2) % 2, tp % 2
    y = yhi * 2 + ylo
    here = {"x": x, "y": y, "z": z}

    def device(at, c):
        return (
            (at["y"] % 2) * 4 + at["z"],
            at["x"] * 4 + (at["y"] // 2) * 2 + c,
        )

    def moved(axis, step):
        at = dict(here)
        at[axis] = (here[axis] + step) % 4
        return at

    right = {a: device(moved(a, 1), core) for a in "xyz"}
    left = {a: device(moved(a, 3), core) for a in "xyz"}
    far = {a: device(moved(a, 2), core) for a in "xyz"}
    sibling = device(here, 1 - core)

    small = [
        pltpu.make_async_copy(src, dst, in_sem.at[n])
        for n, (src, dst) in enumerate(
            (
                (gi_ref, gi),
                (ui_ref, ui),
                (di_ref, di),
                (gi_ref, giv),
                (ui_ref, uiv),
                (di_ref, div),
                (gs_ref, gsv),
                (us_ref, usv),
                (ds_ref, dsv),
            )
        )
    ]

    def load(src):
        return pltpu.make_async_copy(src, stage.at[pl.ds(0, KB)], ld_sem)

    barrier = pltpu.get_barrier_semaphore()
    partners = list(right.values()) + list(left.values()) + list(far.values()) + [sibling]
    for other in partners:
        pl.semaphore_signal(barrier, inc=1, device_id=other, device_id_type=MESH)
    for copy in small:
        copy.start()
    load(gb_ref).start()
    for j in range(DC):
        cols = pl.ds(j * BLK, BLK)
        buf[0, j, core, z, y, x] = tok_ref[:, cols]
        buf[1, j, core, z, y, x] = cot_ref[:, cols]
    pl.semaphore_wait(barrier, len(partners))

    def region(q, third, phase, along, lo, hi):
        axes = ORDERS[third]
        idx = []
        for a in ("z", "y", "x"):
            if a in axes[:phase]:
                idx.append(slice(None))
            elif a == axes[phase]:
                idx.append(along)
            else:
                idx.append(here[a])
        return buf.at[(q, pl.ds(lo, hi - lo), core, *idx)]

    def ag_copy(q, third, phase, k):
        lo, mid_col, hi = THIRDS[third]
        axis = ORDERS[third][phase]
        own = here[axis]
        if phase < 2:
            along, cols, to = own, (lo, hi), (right, left, far)[k]
        else:
            along, cols, to = (
                (own, (lo, mid_col), right),
                (own, (mid_col, hi), left),
                (own, (mid_col, hi), right),
                (own, (lo, mid_col), left),
                ((own + 3) % 4, (lo, mid_col), right),
                ((own + 1) % 4, (mid_col, hi), left),
            )[k]
        ref = region(q, third, phase, along, *cols)
        return pltpu.make_async_remote_copy(
            src_ref=ref,
            dst_ref=ref,
            send_sem=ag_send.at[q, third, phase, k],
            recv_sem=ag_recv.at[q, third, phase, k],
            device_id=to[axis],
            device_id_type=MESH,
        )

    def sib_copy(q, third, k):
        lo, _, hi = THIRDS[third]
        axis = ORDERS[third][2]
        ref = region(q, third, 2, (here[axis] + k) % 4, lo, hi)
        return pltpu.make_async_remote_copy(
            src_ref=ref,
            dst_ref=ref,
            send_sem=sib_send.at[q, third, k],
            recv_sem=sib_recv.at[q, third, k],
            device_id=sibling,
            device_id_type=MESH,
        )

    def ag_start(q, phase):
        for k in range(4 if phase == 2 else 3):
            for third in range(3):
                ag_copy(q, third, phase, k).start()

    def ag_wait(q, phase):
        for third in range(3):
            for k in range(3):
                ag_copy(q, third, phase, k).wait_recv()

    def ag_forward(q):
        for third in range(3):
            ag_copy(q, third, 2, 0).wait_recv()
            ag_copy(q, third, 2, 4).start()
            ag_copy(q, third, 2, 1).wait_recv()
            ag_copy(q, third, 2, 5).start()

    def ag_direct(q):
        for third in range(3):
            ag_copy(q, third, 2, 2).wait_recv()
            ag_copy(q, third, 2, 3).wait_recv()

    def ag_far(q):
        for third in range(3):
            ag_copy(q, third, 2, 4).wait_recv()
            ag_copy(q, third, 2, 5).wait_recv()

    def sib_start(q, k):
        for third in range(3):
            sib_copy(q, third, k).start()

    def sib_wait(q):
        for third in range(3):
            for k in range(4):
                sib_copy(q, third, k).wait_recv()

    def ag_finish(q):
        for third in range(3):
            for phase in range(3):
                for k in range(6 if phase == 2 else 3):
                    ag_copy(q, third, phase, k).wait_send()
            for k in range(4):
                sib_copy(q, third, k).wait_send()

    def find_blocks():
        for n in range(3):
            taken[n] = 0

        @pl.loop(0, DC)
        def _(r):
            for c in range(FC):
                number = r * FC + c
                for n, ids in enumerate((gi, ui, di)):
                    at = jnp.minimum(taken[n], KB - 1)
                    hit = ids[0, at] == number
                    where[n, number] = jnp.where(hit, at, KB)
                    taken[n] = taken[n] + hit.astype(jnp.int32)

    def spread(n, per, store, lo, hi):
        @pl.loop(lo, hi)
        def _(r):
            for c in range(per):
                store(r, c, stage[where[n, r * per + c]])

    def block_rows(r):
        return pl.ds(pl.multiple_of(r * BLK, BLK), BLK)

    def store_gate(r, c, block):
        wgu[c, block_rows(r), pl.ds(0, BLK)] = block

    def store_up(r, c, block):
        wgu[c, block_rows(r), pl.ds(BLK, BLK)] = block

    def store_down(r, c, block):
        wd[block_rows(r), pl.ds(c * BLK, BLK)] = block

    flat = buf.reshape(2, DC, TOK, BLK)

    def rows_of(q, rows):
        return jnp.concatenate([flat[q, j, rows, :] for j in range(DC)], axis=1)

    def forward_cols(lo, hi, start, size):
        @pl.loop(lo, hi)
        def _(c):
            for rows in [pl.ds(start, size)]:
                both = jnp.dot(rows_of(0, rows), wgu[c], preferred_element_type=F32)
                gate, up = both[:, :BLK], both[:, BLK:]
                sigma = 1.0 / (1.0 + jnp.exp(-gate))
                swish = gate * sigma
                hid[c, rows, :] = (swish * up).astype(BF16)
                gpre[2 * c, rows, :] = (up * sigma * (1.0 + gate * (1.0 - sigma))).astype(BF16)
                gpre[2 * c + 1, rows, :] = swish.astype(BF16)

    def backward_cols(start, width):
        for rows in [pl.ds(0, TOK)]:
            w = wd[pl.ds(pl.multiple_of(start * BLK, BLK), width * BLK), :]
            grad = lax.dot_general(
                rows_of(1, rows), w, (((1,), (1,)), ((), ())), preferred_element_type=F32
            )
            for j in range(width):
                piece = grad[:, j * BLK : (j + 1) * BLK]
                for side in range(2):
                    k = 2 * (start + j) + side
                    gpre[k, rows, :] = (gpre[k, rows, :].astype(F32) * piece).astype(BF16)

    def own_rows(ref, *lead):
        runs = []
        for h in range(2):
            for c in range(2):
                at = c * 512 + (z * 4 + h * 2 + ylo) * 32
                rows = pl.ds(pl.multiple_of(at, 32), 32)
                blocks = ref.shape[len(lead)]
                runs.append(
                    jnp.concatenate([ref[(*lead, j, rows)] for j in range(blocks)], axis=1)
                )
        return jnp.concatenate(runs, axis=0)

    def own_backward(start, width):
        w = wd[pl.ds(pl.multiple_of(start * BLK, BLK), width * BLK), :]
        grad = lax.dot_general(
            own_rows(flat, 1), w, (((1,), (1,)), ((), ())), preferred_element_type=F32
        )
        for j in range(width):
            piece = grad[:, j * BLK : (j + 1) * BLK]
            for side in range(2):
                k = 2 * (start + j) + side
                runs = []
                for h in range(2):
                    for c in range(2):
                        at = c * 512 + (z * 4 + h * 2 + ylo) * 32
                        runs.append(gpre[k, pl.ds(pl.multiple_of(at, 32), 32), :])
                slope = jnp.concatenate(runs, axis=0).astype(F32)
                own_g[k] = (slope * piece).astype(BF16)

    def partial_out(o):
        width = 512

        @pl.loop(0, D // width)
        def _(n):
            cols = pl.ds(pl.multiple_of(n * width, width), width)
            if o == 0:
                term = jnp.dot(own_rows(hid), wd[:, cols], preferred_element_type=F32)
            else:
                term = lax.dot_general(
                    jnp.concatenate([own_g[k] for k in range(2 * FC)], axis=1),
                    jnp.concatenate([wgu[c, cols, :] for c in range(FC)], axis=1),
                    (((1,), (1,)), ((), ())),
                    preferred_element_type=F32,
                )
            part[o, :, :, :, :, cols] = term.astype(BF16).reshape(2, 2, 4, 8, width)

    def rs_copy(o, k):
        if k == 0:
            src, dst, to = part.at[o, :, 1 - core], got1.at[o], sibling
        elif k < 4:
            at = moved("x", k)
            src, dst, to = part.at[o, :, core, at["x"]], got2.at[o, k - 1], device(at, core)
        else:
            src, dst, to = mid.at[o, 1 - yhi], got3.at[o], far["y"]
        return pltpu.make_async_remote_copy(
            src_ref=src,
            dst_ref=dst,
            send_sem=rs_send.at[o, k],
            recv_sem=rs_recv.at[o, k],
            device_id=to,
            device_id_type=MESH,
        )

    def rs_one(o):
        rs_copy(o, 0).start()

    def rs_two(o):
        rs_copy(o, 0).wait_recv()
        for h in range(2):
            for w in range(4):
                part[o, h, core, w] = (
                    part[o, h, core, w].astype(F32) + got1[o, h, w].astype(F32)
                ).astype(BF16)
        for k in (2, 1, 3):
            rs_copy(o, k).start()

    def rs_three(o):
        for k in range(1, 4):
            rs_copy(o, k).wait_recv()
        for h in range(2):
            total = part[o, h, core, x].astype(F32)
            for k in range(3):
                total = total + got2[o, k, h].astype(F32)
            mid[o, h] = total.astype(BF16)
        rs_copy(o, 4).start()

    def row_copy(o):
        return pltpu.make_async_copy(rows_out.at[o], (lo_ref, tg_ref)[o], out_sem.at[o])

    def rs_four(o):
        rs_copy(o, 4).wait_recv()
        rows_out[o] = (mid[o, yhi].astype(F32) + got3[o].astype(F32)).astype(BF16)
        row_copy(o).start()
        for k in range(5):
            rs_copy(o, k).wait_send()

    def pick_slots():
        @pl.loop(0, CAP)
        def _(v):
            mine = dp * CAP + v
            for n, (ids, slots) in enumerate(((giv, gsv), (uiv, usv), (div, dsv))):
                picks[n, v] = jnp.sum(jnp.where(slots[...] == mine, ids[...] + 1, 0))

    factor = 1.0 / math.sqrt(TOK)

    def block_grad(left, right, weight):
        return (
            lax.dot_general(left, right, (((0,), (0,)), ((), ())), preferred_element_type=F32)
            * weight
        )

    def grads(lo, hi):
        @pl.loop(lo, hi)
        def _(v):
            for n in range(3):
                number = picks[n, v]
                block = jnp.maximum(number - 1, 0)
                weight = jnp.where(number > 0, factor, 0.0)
                if n < 2:
                    left = buf[0, block // FC].reshape(TOK, BLK)
                    right = gpre[2 * (block % FC) + n]
                else:
                    left = hid[block // DC]
                    right = buf[1, block % DC].reshape(TOK, BLK)
                grad_out[n, v] = block_grad(left, right, weight)

    def grad_copy(n):
        return pltpu.make_async_copy(grad_out.at[n], (gg_ref, ug_ref, dg_ref)[n], out_sem.at[2 + n])

    mine, other = core * 512, (1 - core) * 512
    ag_start(0, 0)
    stage[KB] = jnp.zeros((BLK, BLK), BF16)
    for copy in small:
        copy.wait()
    find_blocks()
    ag_wait(0, 0)
    ag_start(0, 1)
    ag_start(1, 0)
    load(gb_ref).wait()
    spread(0, FC, store_gate, 0, DC)
    load(ub_ref).start()
    ag_wait(0, 1)
    ag_start(0, 2)
    ag_wait(1, 0)
    ag_start(1, 1)
    sib_start(0, 0)
    load(ub_ref).wait()
    spread(1, FC, store_up, 0, DC)
    load(db_ref).start()
    ag_forward(0)
    ag_wait(1, 1)
    load(db_ref).wait()
    spread(2, DC, store_down, 0, 4)
    ag_direct(0)
    ag_start(1, 2)
    sib_start(0, 1)
    sib_start(0, 3)
    sib_start(1, 0)
    spread(2, DC, store_down, 4, FC)
    pick_slots()
    ag_far(0)
    sib_start(0, 2)
    forward_cols(0, 3, pl.multiple_of(mine, 512), 512)
    ag_forward(1)
    sib_wait(0)
    forward_cols(0, 3, pl.multiple_of(other, 512), 512)
    forward_cols(3, FC, 0, TOK)
    ag_direct(1)
    sib_start(1, 1)
    sib_start(1, 3)
    ag_far(1)
    sib_start(1, 2)
    partial_out(0)
    rs_one(0)
    sib_wait(1)

    @pl.loop(0, 3)
    def _(c):
        own_backward(2 * c, 2)

    own_backward(FC - 1, 1)
    rs_two(0)
    partial_out(1)
    rs_one(1)
    rs_three(0)

    @pl.loop(0, 2)
    def _(c):
        backward_cols(2 * c, 2)

    rs_two(1)
    rs_four(0)

    @pl.loop(2, 3)
    def _(c):
        backward_cols(2 * c, 2)

    backward_cols(FC - 1, 1)
    rs_three(1)
    grads(0, 10)
    rs_four(1)
    grads(10, CAP)
    for n in range(3):
        grad_copy(n).start()
    ag_finish(0)
    ag_finish(1)
    for o in range(2):
        row_copy(o).wait()
    for n in range(3):
        grad_copy(n).wait()


def copy_body(*refs):
    for source, target in zip(refs[:5], refs[5:]):
        target[...] = source[...]


def local(
    tokens,
    out_grad,
    gate_blocks,
    up_blocks,
    down_blocks,
    gate_index,
    up_index,
    down_index,
    gate_slot,
    up_slot,
    down_slot,
):
    hbm = pl.BlockSpec(memory_space=pl.ANY)
    vmem = pl.BlockSpec(memory_space=pltpu.VMEM)
    rows = jax.ShapeDtypeStruct((8, D), BF16)
    owned = jax.ShapeDtypeStruct((CAP, BLK, BLK), F32)
    shapes = (rows, rows, owned, owned, owned)
    results = pl.pallas_call(
        kernel_body,
        out_shape=shapes,
        in_specs=[vmem, vmem] + [hbm] * 9,
        out_specs=(hbm,) * 5,
        scratch_shapes=[pltpu.SMEM((1, KB), jnp.int32)] * 3
        + [pltpu.VMEM((1, KB), jnp.int32)] * 6
        + [
            pltpu.SMEM((3, CAP), jnp.int32),
            pltpu.SMEM((3,), jnp.int32),
            pltpu.SMEM((3, NBLK), jnp.int32),
            pltpu.VMEM((2, DC, 2, 4, 4, 4, 8, BLK), BF16),
            pltpu.VMEM((FC, D, 2 * BLK), BF16),
            pltpu.VMEM((FDEV, D), BF16),
            pltpu.VMEM((KB + 1, BLK, BLK), BF16),
            pltpu.VMEM((FC, TOK, BLK), BF16),
            pltpu.VMEM((2 * FC, TOK, BLK), BF16),
            pltpu.VMEM((2 * FC, BLK, BLK), BF16),
            pltpu.VMEM((2, 2, 2, 4, 8, D), BF16),
            pltpu.VMEM((2, 2, 4, 8, D), BF16),
            pltpu.VMEM((2, 3, 2, 8, D), BF16),
            pltpu.VMEM((2, 2, 8, D), BF16),
            pltpu.VMEM((2, 8, D), BF16),
            pltpu.VMEM((2, 8, D), BF16),
            pltpu.VMEM((3, CAP, BLK, BLK), F32),
            pltpu.SemaphoreType.DMA((9,)),
            pltpu.SemaphoreType.DMA,
            pltpu.SemaphoreType.DMA((5,)),
            pltpu.SemaphoreType.DMA((2, 3, 3, 6)),
            pltpu.SemaphoreType.DMA((2, 3, 3, 6)),
            pltpu.SemaphoreType.DMA((2, 3, 4)),
            pltpu.SemaphoreType.DMA((2, 3, 4)),
            pltpu.SemaphoreType.DMA((2, 5)),
            pltpu.SemaphoreType.DMA((2, 5)),
        ],
        compiler_params=pltpu.CompilerParams(
            collective_id=0, has_side_effects=True, vmem_limit_bytes=62 * 1024 * 1024
        ),
    )(
        tokens,
        out_grad,
        gate_blocks,
        up_blocks,
        down_blocks,
        gate_index,
        up_index,
        down_index,
        gate_slot,
        up_slot,
        down_slot,
    )
    lo, tg, gg, ug, dg = pl.pallas_call(
        copy_body,
        out_shape=shapes,
        in_specs=[vmem] * 5,
        out_specs=(vmem,) * 5,
    )(*results)
    return lo, tg, gg[None], ug[None], dg[None]


def solution(mesh):
    in_specs = (
        P(("dp", "tensor"), None),
        P(("dp", "tensor"), None),
        P("tensor", None, None),
        P("tensor", None, None),
        P("tensor", None, None),
        P("tensor", None),
        P("tensor", None),
        P("tensor", None),
        P("tensor", None),
        P("tensor", None),
        P("tensor", None),
    )
    out_specs = (
        P(("dp", "tensor"), None),
        P(("dp", "tensor"), None),
        P("tensor", "dp", None, None),
        P("tensor", "dp", None, None),
        P("tensor", "dp", None, None),
    )
    return jax.shard_map(local, mesh=mesh, in_specs=in_specs, out_specs=out_specs, check_vma=False)
```

```python
import functools
import math

import jax
import jax.numpy as jnp
from jax import lax
from jax.experimental import pallas as pl
from jax.experimental.pallas import tpu as pltpu
from jax.sharding import PartitionSpec as P

MESH = pl.DeviceIdType.MESH
D = 4096
BLK = 128
DC = 32
FC = 7
FDEV = 896
KB = 112
NBLK = 224
CAP = 17
TOK = 1024
F32 = jnp.float32
BF16 = jnp.bfloat16

THIRDS = ((0, 6, 12), (12, 17, 22), (22, 27, 32))
ORDERS = (("x", "y", "z"), ("y", "z", "x"), ("z", "x", "y"))


def kernel_body(
    tok_ref,
    cot_ref,
    gb_ref,
    ub_ref,
    db_ref,
    gi_ref,
    ui_ref,
    di_ref,
    gs_ref,
    us_ref,
    ds_ref,
    lo_ref,
    tg_ref,
    gg_ref,
    ug_ref,
    dg_ref,
    gi,
    ui,
    di,
    giv,
    uiv,
    div,
    gsv,
    usv,
    dsv,
    picks,
    taken,
    where,
    buf,
    wgu,
    wd,
    stage,
    hid,
    gpre,
    own_g,
    part,
    got1,
    got2,
    mid,
    got3,
    in_sem,
    ld_sem,
    ag_send,
    ag_recv,
    sib_send,
    sib_recv,
    rs_send,
    rs_recv,
):
    dp = lax.axis_index("dp")
    tp = lax.axis_index("tensor")
    ylo, z = dp // 4, dp % 4
    x, yhi, core = tp // 4, (tp // 2) % 2, tp % 2
    y = yhi * 2 + ylo
    here = {"x": x, "y": y, "z": z}

    def device(at, c):
        return (
            (at["y"] % 2) * 4 + at["z"],
            at["x"] * 4 + (at["y"] // 2) * 2 + c,
        )

    def moved(axis, step):
        at = dict(here)
        at[axis] = (here[axis] + step) % 4
        return at

    right = {a: device(moved(a, 1), core) for a in "xyz"}
    left = {a: device(moved(a, 3), core) for a in "xyz"}
    far = {a: device(moved(a, 2), core) for a in "xyz"}
    sibling = device(here, 1 - core)

    small = [
        pltpu.make_async_copy(src, dst, in_sem.at[n])
        for n, (src, dst) in enumerate(
            (
                (gi_ref, gi),
                (ui_ref, ui),
                (di_ref, di),
                (gi_ref, giv),
                (ui_ref, uiv),
                (di_ref, div),
                (gs_ref, gsv),
                (us_ref, usv),
                (ds_ref, dsv),
            )
        )
    ]

    def load(src):
        return pltpu.make_async_copy(src, stage.at[pl.ds(0, KB)], ld_sem)

    barrier = pltpu.get_barrier_semaphore()
    partners = list(right.values()) + list(left.values()) + list(far.values()) + [sibling]
    for other in partners:
        pl.semaphore_signal(barrier, inc=1, device_id=other, device_id_type=MESH)
    for copy in small:
        copy.start()
    load(gb_ref).start()
    for j in range(DC):
        cols = pl.ds(j * BLK, BLK)
        buf[0, j, core, z, y, x] = tok_ref[:, cols]
        buf[1, j, core, z, y, x] = cot_ref[:, cols]
    pl.semaphore_wait(barrier, len(partners))

    def region(q, third, phase, along, lo, hi):
        axes = ORDERS[third]
        idx = []
        for a in ("z", "y", "x"):
            if a in axes[:phase]:
                idx.append(slice(None))
            elif a == axes[phase]:
                idx.append(along)
            else:
                idx.append(here[a])
        return buf.at[(q, pl.ds(lo, hi - lo), core, *idx)]

    def ag_copy(q, third, phase, k):
        lo, mid_col, hi = THIRDS[third]
        axis = ORDERS[third][phase]
        own = here[axis]
        if phase < 2:
            along, cols, to = own, (lo, hi), (right, left, far)[k]
        else:
            along, cols, to = (
                (own, (lo, mid_col), right),
                (own, (mid_col, hi), left),
                (own, (mid_col, hi), right),
                (own, (lo, mid_col), left),
                ((own + 3) % 4, (lo, mid_col), right),
                ((own + 1) % 4, (mid_col, hi), left),
            )[k]
        ref = region(q, third, phase, along, *cols)
        return pltpu.make_async_remote_copy(
            src_ref=ref,
            dst_ref=ref,
            send_sem=ag_send.at[q, third, phase, k],
            recv_sem=ag_recv.at[q, third, phase, k],
            device_id=to[axis],
            device_id_type=MESH,
        )

    def sib_copy(q, third, k):
        lo, _, hi = THIRDS[third]
        axis = ORDERS[third][2]
        ref = region(q, third, 2, (here[axis] + k) % 4, lo, hi)
        return pltpu.make_async_remote_copy(
            src_ref=ref,
            dst_ref=ref,
            send_sem=sib_send.at[q, third, k],
            recv_sem=sib_recv.at[q, third, k],
            device_id=sibling,
            device_id_type=MESH,
        )

    def ag_start(q, phase):
        for k in range(4 if phase == 2 else 3):
            for third in range(3):
                ag_copy(q, third, phase, k).start()

    def ag_wait(q, phase):
        for third in range(3):
            for k in range(3):
                ag_copy(q, third, phase, k).wait_recv()

    def ag_forward(q):
        for third in range(3):
            ag_copy(q, third, 2, 0).wait_recv()
            ag_copy(q, third, 2, 4).start()
            ag_copy(q, third, 2, 1).wait_recv()
            ag_copy(q, third, 2, 5).start()

    def ag_direct(q):
        for third in range(3):
            ag_copy(q, third, 2, 2).wait_recv()
            ag_copy(q, third, 2, 3).wait_recv()

    def ag_far(q):
        for third in range(3):
            ag_copy(q, third, 2, 4).wait_recv()
            ag_copy(q, third, 2, 5).wait_recv()

    def sib_start(q, k):
        for third in range(3):
            sib_copy(q, third, k).start()

    def sib_wait(q):
        for third in range(3):
            for k in range(4):
                sib_copy(q, third, k).wait_recv()

    def ag_finish(q):
        for third in range(3):
            for phase in range(3):
                for k in range(6 if phase == 2 else 3):
                    ag_copy(q, third, phase, k).wait_send()
            for k in range(4):
                sib_copy(q, third, k).wait_send()

    def find_blocks():
        for n in range(3):
            taken[n] = 0

        @pl.loop(0, DC)
        def _(r):
            for c in range(FC):
                number = r * FC + c
                for n, ids in enumerate((gi, ui, di)):
                    at = jnp.minimum(taken[n], KB - 1)
                    hit = ids[0, at] == number
                    where[n, number] = jnp.where(hit, at, KB)
                    taken[n] = taken[n] + hit.astype(jnp.int32)

    def spread(n, per, store, lo, hi):
        @pl.loop(lo, hi)
        def _(r):
            for c in range(per):
                store(r, c, stage[where[n, r * per + c]])

    def block_rows(r):
        return pl.ds(pl.multiple_of(r * BLK, BLK), BLK)

    def store_gate(r, c, block):
        wgu[c, block_rows(r), pl.ds(0, BLK)] = block

    def store_up(r, c, block):
        wgu[c, block_rows(r), pl.ds(BLK, BLK)] = block

    def store_down(r, c, block):
        wd[block_rows(r), pl.ds(c * BLK, BLK)] = block

    flat = buf.reshape(2, DC, TOK, BLK)

    def rows_of(q, rows):
        return jnp.concatenate([flat[q, j, rows, :] for j in range(DC)], axis=1)

    def forward_cols(lo, hi, start, size, then):
        @pl.loop(lo, hi)
        def _(c):
            for rows in [pl.ds(start, size)]:
                both = jnp.dot(rows_of(0, rows), wgu[c], preferred_element_type=F32)
                gate, up = both[:, :BLK], both[:, BLK:]
                sigma = 1.0 / (1.0 + jnp.exp(-gate))
                swish = gate * sigma
                hid[c, rows, :] = (swish * up).astype(BF16)
                gpre[2 * c, rows, :] = (up * sigma * (1.0 + gate * (1.0 - sigma))).astype(BF16)
                gpre[2 * c + 1, rows, :] = swish.astype(BF16)

            for last, step in then.items():
                pl.when(c == last)(step)

    def backward_cols(start, width):
        for rows in [pl.ds(0, TOK)]:
            w = wd[pl.ds(pl.multiple_of(start * BLK, BLK), width * BLK), :]
            grad = lax.dot_general(
                rows_of(1, rows), w, (((1,), (1,)), ((), ())), preferred_element_type=F32
            )
            for j in range(width):
                piece = grad[:, j * BLK : (j + 1) * BLK]
                for side in range(2):
                    k = 2 * (start + j) + side
                    gpre[k, rows, :] = (gpre[k, rows, :].astype(F32) * piece).astype(BF16)

    def own_rows(ref, *lead):
        runs = []
        for h in range(2):
            for c in range(2):
                at = c * 512 + (z * 4 + h * 2 + ylo) * 32
                rows = pl.ds(pl.multiple_of(at, 32), 32)
                blocks = ref.shape[len(lead)]
                runs.append(
                    jnp.concatenate([ref[(*lead, j, rows)] for j in range(blocks)], axis=1)
                )
        return jnp.concatenate(runs, axis=0)

    def own_backward(start, width):
        w = wd[pl.ds(pl.multiple_of(start * BLK, BLK), width * BLK), :]
        grad = lax.dot_general(
            own_rows(flat, 1), w, (((1,), (1,)), ((), ())), preferred_element_type=F32
        )
        for j in range(width):
            piece = grad[:, j * BLK : (j + 1) * BLK]
            for side in range(2):
                k = 2 * (start + j) + side
                runs = []
                for h in range(2):
                    for c in range(2):
                        at = c * 512 + (z * 4 + h * 2 + ylo) * 32
                        runs.append(gpre[k, pl.ds(pl.multiple_of(at, 32), 32), :])
                slope = jnp.concatenate(runs, axis=0).astype(F32)
                own_g[k] = (slope * piece).astype(BF16)

    def partial_out(o):
        width = 512

        @pl.loop(0, D // width)
        def _(n):
            cols = pl.ds(pl.multiple_of(n * width, width), width)
            if o == 0:
                term = jnp.dot(own_rows(hid), wd[:, cols], preferred_element_type=F32)
            else:
                term = lax.dot_general(
                    jnp.concatenate([own_g[k] for k in range(2 * FC)], axis=1),
                    jnp.concatenate([wgu[c, cols, :] for c in range(FC)], axis=1),
                    (((1,), (1,)), ((), ())),
                    preferred_element_type=F32,
                )
            part[o, :, :, :, :, cols] = term.astype(BF16).reshape(2, 2, 4, 8, width)

    def rs_copy(o, k):
        if k == 0:
            src, dst, to = part.at[o, :, 1 - core], got1.at[o], sibling
        elif k < 4:
            at = moved("x", k)
            src, dst, to = part.at[o, :, core, at["x"]], got2.at[o, k - 1], device(at, core)
        else:
            src, dst, to = mid.at[o, 1 - yhi], got3.at[o], far["y"]
        return pltpu.make_async_remote_copy(
            src_ref=src,
            dst_ref=dst,
            send_sem=rs_send.at[o, k],
            recv_sem=rs_recv.at[o, k],
            device_id=to,
            device_id_type=MESH,
        )

    def rs_one(o):
        rs_copy(o, 0).start()

    def rs_two(o):
        rs_copy(o, 0).wait_recv()
        for h in range(2):
            for w in range(4):
                part[o, h, core, w] = (
                    part[o, h, core, w].astype(F32) + got1[o, h, w].astype(F32)
                ).astype(BF16)
        for k in (2, 1, 3):
            rs_copy(o, k).start()

    def rs_three(o):
        for k in range(1, 4):
            rs_copy(o, k).wait_recv()
        for h in range(2):
            total = part[o, h, core, x].astype(F32)
            for k in range(3):
                total = total + got2[o, k, h].astype(F32)
            mid[o, h] = total.astype(BF16)
        rs_copy(o, 4).start()

    def rs_four(o):
        rs_copy(o, 4).wait_recv()
        total = mid[o, yhi].astype(F32) + got3[o].astype(F32)
        (lo_ref, tg_ref)[o][...] = total.astype(BF16)
        for k in range(5):
            rs_copy(o, k).wait_send()

    def pick_slots():
        @pl.loop(0, CAP)
        def _(v):
            mine = dp * CAP + v
            for n, (ids, slots) in enumerate(((giv, gsv), (uiv, usv), (div, dsv))):
                picks[n, v] = jnp.sum(jnp.where(slots[...] == mine, ids[...] + 1, 0))

    factor = 1.0 / math.sqrt(TOK)

    def block_grad(left, right, weight):
        return (
            lax.dot_general(left, right, (((0,), (0,)), ((), ())), preferred_element_type=F32)
            * weight
        )

    def grads(lo, hi):
        @pl.loop(lo, hi)
        def _(v):
            for n in range(3):
                number = picks[n, v]
                block = jnp.maximum(number - 1, 0)
                weight = jnp.where(number > 0, factor, 0.0)
                if n < 2:
                    left = buf[0, block // FC].reshape(TOK, BLK)
                    right = gpre[2 * (block % FC) + n]
                else:
                    left = hid[block // DC]
                    right = buf[1, block % DC].reshape(TOK, BLK)
                (gg_ref, ug_ref, dg_ref)[n][v] = block_grad(left, right, weight)

    mine, other = core * 512, (1 - core) * 512
    ag_start(0, 0)
    ag_start(1, 0)
    stage[KB] = jnp.zeros((BLK, BLK), BF16)
    for copy in small:
        copy.wait()
    find_blocks()
    ag_wait(0, 0)
    ag_start(0, 1)
    ag_wait(1, 0)
    ag_start(1, 1)
    load(gb_ref).wait()
    spread(0, FC, store_gate, 0, DC)
    load(ub_ref).start()
    ag_wait(0, 1)
    ag_start(0, 2)
    ag_wait(1, 1)
    sib_start(0, 0)
    load(ub_ref).wait()
    spread(1, FC, store_up, 0, DC)
    load(db_ref).start()
    ag_forward(0)
    ag_start(1, 2)
    load(db_ref).wait()
    spread(2, DC, store_down, 0, 4)
    ag_direct(0)
    sib_start(0, 1)
    sib_start(0, 3)
    sib_start(1, 0)
    spread(2, DC, store_down, 4, FC)
    pick_slots()
    ag_far(0)
    sib_start(0, 2)
    forward_cols(0, 3, pl.multiple_of(mine, 512), 512, {})
    ag_forward(1)
    sib_wait(0)
    forward_cols(0, 3, pl.multiple_of(other, 512), 512, {})

    def cots_direct():
        ag_direct(1)
        sib_start(1, 1)
        sib_start(1, 3)

    def cots_far():
        ag_far(1)
        sib_start(1, 2)

    forward_cols(3, FC, 0, TOK, {3: cots_direct, 5: cots_far})
    partial_out(0)
    rs_one(0)
    sib_wait(1)

    @pl.loop(0, 3)
    def _(c):
        own_backward(2 * c, 2)

    own_backward(FC - 1, 1)
    partial_out(1)
    rs_two(0)
    rs_one(1)

    @pl.loop(0, 3)
    def _(c):
        backward_cols(2 * c, 2)

        @pl.when(c == 1)
        def _():
            rs_two(1)

    rs_three(0)
    backward_cols(FC - 1, 1)
    grads(0, 7)
    rs_three(1)
    rs_four(0)
    grads(7, CAP)
    rs_four(1)
    ag_finish(0)
    ag_finish(1)


def copy_body(*refs):
    sem = refs[10]
    copies = [
        pltpu.make_async_copy(source, target, sem.at[n])
        for n, (source, target) in enumerate(zip(refs[:5], refs[5:10]))
    ]
    for copy in copies:
        copy.start()
    for copy in copies:
        copy.wait()


def local(
    tokens,
    out_grad,
    gate_blocks,
    up_blocks,
    down_blocks,
    gate_index,
    up_index,
    down_index,
    gate_slot,
    up_slot,
    down_slot,
):
    hbm = pl.BlockSpec(memory_space=pl.ANY)
    vmem = pl.BlockSpec(memory_space=pltpu.VMEM)
    rows = jax.ShapeDtypeStruct((8, D), BF16)
    owned = jax.ShapeDtypeStruct((CAP, BLK, BLK), F32)
    shapes = (rows, rows, owned, owned, owned)
    results = pl.pallas_call(
        kernel_body,
        out_shape=tuple(pltpu.VMEM(shape.shape, shape.dtype) for shape in shapes),
        in_specs=[vmem, vmem] + [hbm] * 9,
        out_specs=(vmem,) * 5,
        scratch_shapes=[pltpu.SMEM((1, KB), jnp.int32)] * 3
        + [pltpu.VMEM((1, KB), jnp.int32)] * 6
        + [
            pltpu.SMEM((3, CAP), jnp.int32),
            pltpu.SMEM((3,), jnp.int32),
            pltpu.SMEM((3, NBLK), jnp.int32),
            pltpu.VMEM((2, DC, 2, 4, 4, 4, 8, BLK), BF16),
            pltpu.VMEM((FC, D, 2 * BLK), BF16),
            pltpu.VMEM((FDEV, D), BF16),
            pltpu.VMEM((KB + 1, BLK, BLK), BF16),
            pltpu.VMEM((FC, TOK, BLK), BF16),
            pltpu.VMEM((2 * FC, TOK, BLK), BF16),
            pltpu.VMEM((2 * FC, BLK, BLK), BF16),
            pltpu.VMEM((2, 2, 2, 4, 8, D), BF16),
            pltpu.VMEM((2, 2, 4, 8, D), BF16),
            pltpu.VMEM((2, 3, 2, 8, D), BF16),
            pltpu.VMEM((2, 2, 8, D), BF16),
            pltpu.VMEM((2, 8, D), BF16),
            pltpu.SemaphoreType.DMA((9,)),
            pltpu.SemaphoreType.DMA,
            pltpu.SemaphoreType.DMA((2, 3, 3, 6)),
            pltpu.SemaphoreType.DMA((2, 3, 3, 6)),
            pltpu.SemaphoreType.DMA((2, 3, 4)),
            pltpu.SemaphoreType.DMA((2, 3, 4)),
            pltpu.SemaphoreType.DMA((2, 5)),
            pltpu.SemaphoreType.DMA((2, 5)),
        ],
        compiler_params=pltpu.CompilerParams(
            collective_id=0, has_side_effects=True, vmem_limit_bytes=56 * 1024 * 1024
        ),
    )(
        tokens,
        out_grad,
        gate_blocks,
        up_blocks,
        down_blocks,
        gate_index,
        up_index,
        down_index,
        gate_slot,
        up_slot,
        down_slot,
    )
    lo, tg, gg, ug, dg = pl.pallas_call(
        copy_body,
        out_shape=shapes,
        in_specs=[vmem] * 5,
        out_specs=(hbm,) * 5,
        scratch_shapes=[pltpu.SemaphoreType.DMA((5,))],
    )(*results)
    return lo, tg, gg[None], ug[None], dg[None]


def solution(mesh):
    in_specs = (
        P(("dp", "tensor"), None),
        P(("dp", "tensor"), None),
        P("tensor", None, None),
        P("tensor", None, None),
        P("tensor", None, None),
        P("tensor", None),
        P("tensor", None),
        P("tensor", None),
        P("tensor", None),
        P("tensor", None),
        P("tensor", None),
    )
    out_specs = (
        P(("dp", "tensor"), None),
        P(("dp", "tensor"), None),
        P("tensor", "dp", None, None),
        P("tensor", "dp", None, None),
        P("tensor", "dp", None, None),
    )
    return jax.shard_map(local, mesh=mesh, in_specs=in_specs, out_specs=out_specs, check_vma=False)
```

```python
import functools
import math

import jax
import jax.numpy as jnp
from jax import lax
from jax.experimental import pallas as pl
from jax.experimental.pallas import tpu as pltpu
from jax.sharding import PartitionSpec as P

MESH = pl.DeviceIdType.MESH
D = 4096
BLK = 128
DC = 32
FC = 7
FDEV = 896
KB = 112
NBLK = 224
CAP = 17
TOK = 1024
F32 = jnp.float32
BF16 = jnp.bfloat16

THIRDS = ((0, 6, 12), (12, 17, 22), (22, 27, 32))
ORDERS = (("x", "y", "z"), ("y", "z", "x"), ("z", "x", "y"))


def kernel_body(
    tok_ref,
    cot_ref,
    gb_ref,
    ub_ref,
    db_ref,
    gi_ref,
    ui_ref,
    di_ref,
    gs_ref,
    us_ref,
    ds_ref,
    lo_ref,
    tg_ref,
    gg_ref,
    ug_ref,
    dg_ref,
    gi,
    ui,
    di,
    giv,
    uiv,
    div,
    gsv,
    usv,
    dsv,
    picks,
    taken,
    where,
    buf,
    wgu,
    wd,
    stage,
    hid,
    gpre,
    own_g,
    part,
    got1,
    got2,
    mid,
    got3,
    in_sem,
    ld_sem,
    ag_send,
    ag_recv,
    sib_send,
    sib_recv,
    rs_send,
    rs_recv,
):
    dp = lax.axis_index("dp")
    tp = lax.axis_index("tensor")
    ylo, z = dp // 4, dp % 4
    x, yhi, core = tp // 4, (tp // 2) % 2, tp % 2
    y = yhi * 2 + ylo
    here = {"x": x, "y": y, "z": z}

    def device(at, c):
        return (
            (at["y"] % 2) * 4 + at["z"],
            at["x"] * 4 + (at["y"] // 2) * 2 + c,
        )

    def moved(axis, step):
        at = dict(here)
        at[axis] = (here[axis] + step) % 4
        return at

    right = {a: device(moved(a, 1), core) for a in "xyz"}
    left = {a: device(moved(a, 3), core) for a in "xyz"}
    far = {a: device(moved(a, 2), core) for a in "xyz"}
    sibling = device(here, 1 - core)

    small = [
        pltpu.make_async_copy(src, dst, in_sem.at[n])
        for n, (src, dst) in enumerate(
            (
                (gi_ref, gi),
                (ui_ref, ui),
                (di_ref, di),
                (gi_ref, giv),
                (ui_ref, uiv),
                (di_ref, div),
                (gs_ref, gsv),
                (us_ref, usv),
                (ds_ref, dsv),
            )
        )
    ]

    def load(src):
        return pltpu.make_async_copy(src, stage.at[pl.ds(0, KB)], ld_sem)

    barrier = pltpu.get_barrier_semaphore()
    partners = list(right.values()) + list(left.values()) + list(far.values()) + [sibling]
    for other in partners:
        pl.semaphore_signal(barrier, inc=1, device_id=other, device_id_type=MESH)
    for copy in small:
        copy.start()
    load(gb_ref).start()
    for j in range(DC):
        cols = pl.ds(j * BLK, BLK)
        buf[0, j, core, z, y, x] = tok_ref[:, cols]
        buf[1, j, core, z, y, x] = cot_ref[:, cols]
    pl.semaphore_wait(barrier, len(partners))

    def region(q, third, phase, along, lo, hi):
        axes = ORDERS[third]
        idx = []
        for a in ("z", "y", "x"):
            if a in axes[:phase]:
                idx.append(slice(None))
            elif a == axes[phase]:
                idx.append(along)
            else:
                idx.append(here[a])
        return buf.at[(q, pl.ds(lo, hi - lo), core, *idx)]

    def ag_copy(q, third, phase, k):
        lo, mid_col, hi = THIRDS[third]
        axis = ORDERS[third][phase]
        own = here[axis]
        if phase < 2:
            along, cols, to = own, (lo, hi), (right, left, far)[k]
        else:
            along, cols, to = (
                (own, (lo, mid_col), right),
                (own, (mid_col, hi), left),
                (own, (mid_col, hi), right),
                (own, (lo, mid_col), left),
                ((own + 3) % 4, (lo, mid_col), right),
                ((own + 1) % 4, (mid_col, hi), left),
            )[k]
        ref = region(q, third, phase, along, *cols)
        return pltpu.make_async_remote_copy(
            src_ref=ref,
            dst_ref=ref,
            send_sem=ag_send.at[q, third, phase, k],
            recv_sem=ag_recv.at[q, third, phase, k],
            device_id=to[axis],
            device_id_type=MESH,
        )

    def sib_copy(q, third, k):
        lo, _, hi = THIRDS[third]
        axis = ORDERS[third][2]
        ref = region(q, third, 2, (here[axis] + k) % 4, lo, hi)
        return pltpu.make_async_remote_copy(
            src_ref=ref,
            dst_ref=ref,
            send_sem=sib_send.at[q, third, k],
            recv_sem=sib_recv.at[q, third, k],
            device_id=sibling,
            device_id_type=MESH,
        )

    def ag_start(q, phase):
        for k in range(4 if phase == 2 else 3):
            for third in range(3):
                ag_copy(q, third, phase, k).start()

    def ag_wait(q, phase):
        for third in range(3):
            for k in range(3):
                ag_copy(q, third, phase, k).wait_recv()

    def ag_forward(q):
        for third in range(3):
            ag_copy(q, third, 2, 0).wait_recv()
            ag_copy(q, third, 2, 4).start()
            ag_copy(q, third, 2, 1).wait_recv()
            ag_copy(q, third, 2, 5).start()

    def ag_direct(q):
        for third in range(3):
            ag_copy(q, third, 2, 2).wait_recv()
            ag_copy(q, third, 2, 3).wait_recv()

    def ag_far(q):
        for third in range(3):
            ag_copy(q, third, 2, 4).wait_recv()
            ag_copy(q, third, 2, 5).wait_recv()

    def sib_start(q, k):
        for third in range(3):
            sib_copy(q, third, k).start()

    def sib_wait(q):
        for third in range(3):
            for k in range(4):
                sib_copy(q, third, k).wait_recv()

    def ag_finish(q):
        for third in range(3):
            for phase in range(3):
                for k in range(6 if phase == 2 else 3):
                    ag_copy(q, third, phase, k).wait_send()
            for k in range(4):
                sib_copy(q, third, k).wait_send()

    def find_blocks():
        for n in range(3):
            taken[n] = 0

        @pl.loop(0, DC)
        def _(r):
            for c in range(FC):
                number = r * FC + c
                for n, ids in enumerate((gi, ui, di)):
                    at = jnp.minimum(taken[n], KB - 1)
                    hit = ids[0, at] == number
                    where[n, number] = jnp.where(hit, at, KB)
                    taken[n] = taken[n] + hit.astype(jnp.int32)

    def spread(n, per, store, lo, hi):
        @pl.loop(lo, hi)
        def _(r):
            for c in range(per):
                store(r, c, stage[where[n, r * per + c]])

    def block_rows(r):
        return pl.ds(pl.multiple_of(r * BLK, BLK), BLK)

    def store_gate(r, c, block):
        wgu[c, block_rows(r), pl.ds(0, BLK)] = block

    def store_up(r, c, block):
        wgu[c, block_rows(r), pl.ds(BLK, BLK)] = block

    def store_down(r, c, block):
        wd[block_rows(r), pl.ds(c * BLK, BLK)] = block

    flat = buf.reshape(2, DC, TOK, BLK)

    def rows_of(q, rows):
        return jnp.concatenate([flat[q, j, rows, :] for j in range(DC)], axis=1)

    def forward_cols(lo, hi, start, size, then):
        @pl.loop(lo, hi)
        def _(c):
            for rows in [pl.ds(start, size)]:
                both = jnp.dot(rows_of(0, rows), wgu[c], preferred_element_type=F32)
                gate, up = both[:, :BLK], both[:, BLK:]
                sigma = 1.0 / (1.0 + jnp.exp(-gate))
                swish = gate * sigma
                hid[c, rows, :] = (swish * up).astype(BF16)
                gpre[2 * c, rows, :] = (up * sigma * (1.0 + gate * (1.0 - sigma))).astype(BF16)
                gpre[2 * c + 1, rows, :] = swish.astype(BF16)

            for last, step in then.items():
                pl.when(c == last)(step)

    def backward_cols(start, width):
        for rows in [pl.ds(0, TOK)]:
            w = wd[pl.ds(pl.multiple_of(start * BLK, BLK), width * BLK), :]
            grad = lax.dot_general(
                rows_of(1, rows), w, (((1,), (1,)), ((), ())), preferred_element_type=F32
            )
            for j in range(width):
                piece = grad[:, j * BLK : (j + 1) * BLK]
                for side in range(2):
                    k = 2 * (start + j) + side
                    gpre[k, rows, :] = (gpre[k, rows, :].astype(F32) * piece).astype(BF16)

    def own_rows(ref, *lead):
        runs = []
        for h in range(2):
            for c in range(2):
                at = c * 512 + (z * 4 + h * 2 + ylo) * 32
                rows = pl.ds(pl.multiple_of(at, 32), 32)
                blocks = ref.shape[len(lead)]
                runs.append(
                    jnp.concatenate([ref[(*lead, j, rows)] for j in range(blocks)], axis=1)
                )
        return jnp.concatenate(runs, axis=0)

    def own_backward(start, width):
        w = wd[pl.ds(pl.multiple_of(start * BLK, BLK), width * BLK), :]
        grad = lax.dot_general(
            own_rows(flat, 1), w, (((1,), (1,)), ((), ())), preferred_element_type=F32
        )
        for j in range(width):
            piece = grad[:, j * BLK : (j + 1) * BLK]
            for side in range(2):
                k = 2 * (start + j) + side
                runs = []
                for h in range(2):
                    for c in range(2):
                        at = c * 512 + (z * 4 + h * 2 + ylo) * 32
                        runs.append(gpre[k, pl.ds(pl.multiple_of(at, 32), 32), :])
                slope = jnp.concatenate(runs, axis=0).astype(F32)
                own_g[k] = (slope * piece).astype(BF16)

    def partial_out(o):
        width = 512

        @pl.loop(0, D // width)
        def _(n):
            cols = pl.ds(pl.multiple_of(n * width, width), width)
            if o == 0:
                term = jnp.dot(own_rows(hid), wd[:, cols], preferred_element_type=F32)
            else:
                term = lax.dot_general(
                    jnp.concatenate([own_g[k] for k in range(2 * FC)], axis=1),
                    jnp.concatenate([wgu[c, cols, :] for c in range(FC)], axis=1),
                    (((1,), (1,)), ((), ())),
                    preferred_element_type=F32,
                )
            part[o, :, :, :, :, cols] = term.astype(BF16).reshape(2, 2, 4, 8, width)

    def rs_copy(o, k):
        if k == 0:
            src, dst, to = part.at[o, :, 1 - core], got1.at[o], sibling
        elif k < 4:
            at = moved("x", k)
            src, dst, to = part.at[o, :, core, at["x"]], got2.at[o, k - 1], device(at, core)
        else:
            src, dst, to = mid.at[o, 1 - yhi], got3.at[o], far["y"]
        return pltpu.make_async_remote_copy(
            src_ref=src,
            dst_ref=dst,
            send_sem=rs_send.at[o, k],
            recv_sem=rs_recv.at[o, k],
            device_id=to,
            device_id_type=MESH,
        )

    def rs_one(o):
        rs_copy(o, 0).start()

    def rs_two(o):
        rs_copy(o, 0).wait_recv()
        for h in range(2):
            for w in range(4):
                part[o, h, core, w] = (
                    part[o, h, core, w].astype(F32) + got1[o, h, w].astype(F32)
                ).astype(BF16)
        for k in (2, 1, 3):
            rs_copy(o, k).start()

    def rs_three(o):
        for k in range(1, 4):
            rs_copy(o, k).wait_recv()
        for h in range(2):
            total = part[o, h, core, x].astype(F32)
            for k in range(3):
                total = total + got2[o, k, h].astype(F32)
            mid[o, h] = total.astype(BF16)
        rs_copy(o, 4).start()

    def rs_four(o):
        rs_copy(o, 4).wait_recv()
        total = mid[o, yhi].astype(F32) + got3[o].astype(F32)
        (lo_ref, tg_ref)[o][...] = total.astype(BF16)
        for k in range(5):
            rs_copy(o, k).wait_send()

    def pick_slots():
        @pl.loop(0, CAP)
        def _(v):
            mine = dp * CAP + v
            for n, (ids, slots) in enumerate(((giv, gsv), (uiv, usv), (div, dsv))):
                picks[n, v] = jnp.sum(jnp.where(slots[...] == mine, ids[...] + 1, 0))

    factor = 1.0 / math.sqrt(TOK)

    def block_grad(left, right, weight):
        return (
            lax.dot_general(left, right, (((0,), (0,)), ((), ())), preferred_element_type=F32)
            * weight
        )

    def grads(lo, hi):
        @pl.loop(lo, hi)
        def _(v):
            for n in range(3):
                number = picks[n, v]
                block = jnp.maximum(number - 1, 0)
                weight = jnp.where(number > 0, factor, 0.0)
                if n < 2:
                    left = buf[0, block // FC].reshape(TOK, BLK)
                    right = gpre[2 * (block % FC) + n]
                else:
                    left = hid[block // DC]
                    right = buf[1, block % DC].reshape(TOK, BLK)
                (gg_ref, ug_ref, dg_ref)[n][v] = block_grad(left, right, weight)

    mine, other = core * 512, (1 - core) * 512
    ag_start(0, 0)
    ag_start(1, 0)
    stage[KB] = jnp.zeros((BLK, BLK), BF16)
    for copy in small:
        copy.wait()
    find_blocks()
    ag_wait(0, 0)
    ag_start(0, 1)
    ag_wait(1, 0)
    ag_start(1, 1)
    load(gb_ref).wait()
    spread(0, FC, store_gate, 0, DC)
    load(ub_ref).start()
    ag_wait(0, 1)
    ag_start(0, 2)
    ag_wait(1, 1)
    sib_start(0, 0)
    load(ub_ref).wait()
    spread(1, FC, store_up, 0, DC)
    load(db_ref).start()
    ag_forward(0)
    ag_start(1, 2)
    load(db_ref).wait()
    spread(2, DC, store_down, 0, 4)
    ag_direct(0)
    sib_start(0, 1)
    sib_start(0, 3)
    sib_start(1, 0)
    spread(2, DC, store_down, 4, FC)
    pick_slots()
    ag_far(0)
    sib_start(0, 2)
    forward_cols(0, 3, pl.multiple_of(mine, 512), 512, {})
    ag_forward(1)
    sib_wait(0)
    forward_cols(0, 3, pl.multiple_of(other, 512), 512, {})

    def cots_direct():
        ag_direct(1)
        sib_start(1, 1)
        sib_start(1, 3)

    def cots_far():
        ag_far(1)
        sib_start(1, 2)

    forward_cols(3, FC, 0, TOK, {3: cots_direct, 5: cots_far})
    partial_out(0)
    rs_one(0)
    sib_wait(1)

    @pl.loop(0, 3)
    def _(c):
        own_backward(2 * c, 2)

    own_backward(FC - 1, 1)
    partial_out(1)
    rs_two(0)
    rs_one(1)

    @pl.loop(0, 3)
    def _(c):
        backward_cols(2 * c, 2)

        @pl.when(c == 1)
        def _():
            rs_two(1)

    rs_three(0)
    backward_cols(FC - 1, 1)
    grads(0, 7)
    rs_three(1)
    rs_four(0)
    grads(7, CAP)
    rs_four(1)
    ag_finish(0)
    ag_finish(1)


def copy_body(*refs):
    sem = refs[10]
    copies = [
        pltpu.make_async_copy(source, target, sem.at[n])
        for n, (source, target) in enumerate(zip(refs[:5], refs[5:10]))
    ]
    for copy in copies:
        copy.start()
    for copy in copies:
        copy.wait()


def local(
    tokens,
    out_grad,
    gate_blocks,
    up_blocks,
    down_blocks,
    gate_index,
    up_index,
    down_index,
    gate_slot,
    up_slot,
    down_slot,
):
    hbm = pl.BlockSpec(memory_space=pl.ANY)
    vmem = pl.BlockSpec(memory_space=pltpu.VMEM)
    rows = jax.ShapeDtypeStruct((8, D), BF16)
    owned = jax.ShapeDtypeStruct((CAP, BLK, BLK), F32)
    shapes = (rows, rows, owned, owned, owned)
    results = pl.pallas_call(
        kernel_body,
        out_shape=tuple(pltpu.VMEM(shape.shape, shape.dtype) for shape in shapes),
        in_specs=[vmem, vmem] + [hbm] * 9,
        out_specs=(vmem,) * 5,
        scratch_shapes=[pltpu.SMEM((1, KB), jnp.int32)] * 3
        + [pltpu.VMEM((1, KB), jnp.int32)] * 6
        + [
            pltpu.SMEM((3, CAP), jnp.int32),
            pltpu.SMEM((3,), jnp.int32),
            pltpu.SMEM((3, NBLK), jnp.int32),
            pltpu.VMEM((2, DC, 2, 4, 4, 4, 8, BLK), BF16),
            pltpu.VMEM((FC, D, 2 * BLK), BF16),
            pltpu.VMEM((FDEV, D), BF16),
            pltpu.VMEM((KB + 1, BLK, BLK), BF16),
            pltpu.VMEM((FC, TOK, BLK), BF16),
            pltpu.VMEM((2 * FC, TOK, BLK), BF16),
            pltpu.VMEM((2 * FC, BLK, BLK), BF16),
            pltpu.VMEM((2, 2, 2, 4, 8, D), BF16),
            pltpu.VMEM((2, 2, 4, 8, D), BF16),
            pltpu.VMEM((2, 3, 2, 8, D), BF16),
            pltpu.VMEM((2, 2, 8, D), BF16),
            pltpu.VMEM((2, 8, D), BF16),
            pltpu.SemaphoreType.DMA((9,)),
            pltpu.SemaphoreType.DMA,
            pltpu.SemaphoreType.DMA((2, 3, 3, 6)),
            pltpu.SemaphoreType.DMA((2, 3, 3, 6)),
            pltpu.SemaphoreType.DMA((2, 3, 4)),
            pltpu.SemaphoreType.DMA((2, 3, 4)),
            pltpu.SemaphoreType.DMA((2, 5)),
            pltpu.SemaphoreType.DMA((2, 5)),
        ],
        compiler_params=pltpu.CompilerParams(
            collective_id=0, has_side_effects=True, vmem_limit_bytes=56 * 1024 * 1024
        ),
    )(
        tokens,
        out_grad,
        gate_blocks,
        up_blocks,
        down_blocks,
        gate_index,
        up_index,
        down_index,
        gate_slot,
        up_slot,
        down_slot,
    )
    lo, tg, gg, ug, dg = pl.pallas_call(
        copy_body,
        out_shape=shapes,
        in_specs=[vmem] * 5,
        out_specs=(hbm,) * 5,
        scratch_shapes=[pltpu.SemaphoreType.DMA((5,))],
    )(*[pltpu.with_memory_space_constraint(r, pltpu.VMEM) for r in results])
    return lo, tg, gg[None], ug[None], dg[None]


def solution(mesh):
    in_specs = (
        P(("dp", "tensor"), None),
        P(("dp", "tensor"), None),
        P("tensor", None, None),
        P("tensor", None, None),
        P("tensor", None, None),
        P("tensor", None),
        P("tensor", None),
        P("tensor", None),
        P("tensor", None),
        P("tensor", None),
        P("tensor", None),
    )
    out_specs = (
        P(("dp", "tensor"), None),
        P(("dp", "tensor"), None),
        P("tensor", "dp", None, None),
        P("tensor", "dp", None, None),
        P("tensor", "dp", None, None),
    )
    return jax.shard_map(local, mesh=mesh, in_specs=in_specs, out_specs=out_specs, check_vma=False)
```

```python
import functools
import math

import jax
import jax.numpy as jnp
from jax import lax
from jax.experimental import pallas as pl
from jax.experimental.pallas import tpu as pltpu
from jax.sharding import PartitionSpec as P

MESH = pl.DeviceIdType.MESH
D = 4096
BLK = 128
DC = 32
FC = 7
FDEV = 896
KB = 112
NBLK = 224
CAP = 17
TOK = 1024
F32 = jnp.float32
BF16 = jnp.bfloat16

THIRDS = ((0, 6, 11), (11, 16, 22), (22, 27, 32))
RELAYED = ((0, 2), (1, 1), (1, 2))
ORDERS = (("x", "y", "z"), ("y", "z", "x"), ("z", "x", "y"))


def kernel_body(
    tok_ref,
    cot_ref,
    gb_ref,
    ub_ref,
    db_ref,
    gi_ref,
    ui_ref,
    di_ref,
    gs_ref,
    us_ref,
    ds_ref,
    lo_ref,
    tg_ref,
    gg_ref,
    ug_ref,
    dg_ref,
    gi,
    ui,
    di,
    giv,
    uiv,
    div,
    gsv,
    usv,
    dsv,
    picks,
    taken,
    where,
    buf,
    wgu,
    wd,
    stage,
    hid,
    gpre,
    own_g,
    part,
    got1,
    got2,
    mid,
    got3,
    in_sem,
    ld_sem,
    ag_send,
    ag_recv,
    sib_send,
    sib_recv,
    rs_send,
    rs_recv,
):
    dp = lax.axis_index("dp")
    tp = lax.axis_index("tensor")
    ylo, z = dp // 4, dp % 4
    x, yhi, core = tp // 4, (tp // 2) % 2, tp % 2
    y = yhi * 2 + ylo
    here = {"x": x, "y": y, "z": z}

    def device(at, c):
        return (
            (at["y"] % 2) * 4 + at["z"],
            at["x"] * 4 + (at["y"] // 2) * 2 + c,
        )

    def moved(axis, step):
        at = dict(here)
        at[axis] = (here[axis] + step) % 4
        return at

    right = {a: device(moved(a, 1), core) for a in "xyz"}
    left = {a: device(moved(a, 3), core) for a in "xyz"}
    far = {a: device(moved(a, 2), core) for a in "xyz"}
    sibling = device(here, 1 - core)

    small = [
        pltpu.make_async_copy(src, dst, in_sem.at[n])
        for n, (src, dst) in enumerate(
            (
                (gi_ref, gi),
                (ui_ref, ui),
                (di_ref, di),
                (gi_ref, giv),
                (ui_ref, uiv),
                (di_ref, div),
                (gs_ref, gsv),
                (us_ref, usv),
                (ds_ref, dsv),
            )
        )
    ]

    def load(src):
        return pltpu.make_async_copy(src, stage.at[pl.ds(0, KB)], ld_sem)

    barrier = pltpu.get_barrier_semaphore()
    partners = list(right.values()) + list(left.values()) + list(far.values()) + [sibling]
    for other in partners:
        pl.semaphore_signal(barrier, inc=1, device_id=other, device_id_type=MESH)
    for copy in small:
        copy.start()
    load(gb_ref).start()
    for j in range(DC):
        cols = pl.ds(j * BLK, BLK)
        buf[0, j, core, z, y, x] = tok_ref[:, cols]
        buf[1, j, core, z, y, x] = cot_ref[:, cols]
    pl.semaphore_wait(barrier, len(partners))

    def region(q, third, phase, along, lo, hi):
        axes = ORDERS[third]
        idx = []
        for a in ("z", "y", "x"):
            if a in axes[:phase]:
                idx.append(slice(None))
            elif a == axes[phase]:
                idx.append(along)
            else:
                idx.append(here[a])
        return buf.at[(q, pl.ds(lo, hi - lo), core, *idx)]

    def ag_copy(q, third, phase, k):
        lo, mid_col, hi = THIRDS[third]
        axis = ORDERS[third][phase]
        own = here[axis]
        if (q, phase) not in RELAYED:
            along, cols, to = own, (lo, hi), (right, left, far)[k]
        else:
            along, cols, to = (
                (own, (lo, mid_col), right),
                (own, (mid_col, hi), left),
                (own, (mid_col, hi), right),
                (own, (lo, mid_col), left),
                ((own + 3) % 4, (lo, mid_col), right),
                ((own + 1) % 4, (mid_col, hi), left),
            )[k]
        ref = region(q, third, phase, along, *cols)
        return pltpu.make_async_remote_copy(
            src_ref=ref,
            dst_ref=ref,
            send_sem=ag_send.at[q, third, phase, k],
            recv_sem=ag_recv.at[q, third, phase, k],
            device_id=to[axis],
            device_id_type=MESH,
        )

    def sib_copy(q, third, k):
        lo, _, hi = THIRDS[third]
        axis = ORDERS[third][2]
        ref = region(q, third, 2, (here[axis] + k) % 4, lo, hi)
        return pltpu.make_async_remote_copy(
            src_ref=ref,
            dst_ref=ref,
            send_sem=sib_send.at[q, third, k],
            recv_sem=sib_recv.at[q, third, k],
            device_id=sibling,
            device_id_type=MESH,
        )

    def ag_start(q, phase):
        for k in range(4 if (q, phase) in RELAYED else 3):
            for third in range(3):
                ag_copy(q, third, phase, k).start()

    def ag_wait(q, phase):
        for third in range(3):
            for k in range(3):
                ag_copy(q, third, phase, k).wait_recv()

    def ag_forward(q, phase=2):
        for third in range(3):
            ag_copy(q, third, phase, 0).wait_recv()
            ag_copy(q, third, phase, 4).start()
            ag_copy(q, third, phase, 1).wait_recv()
            ag_copy(q, third, phase, 5).start()

    def ag_direct(q, phase=2):
        for third in range(3):
            ag_copy(q, third, phase, 2).wait_recv()
            ag_copy(q, third, phase, 3).wait_recv()

    def ag_far(q, phase=2):
        for third in range(3):
            ag_copy(q, third, phase, 4).wait_recv()
            ag_copy(q, third, phase, 5).wait_recv()

    def sib_start(q, k):
        for third in range(3):
            sib_copy(q, third, k).start()

    def sib_wait(q):
        for third in range(3):
            for k in range(4):
                sib_copy(q, third, k).wait_recv()

    def ag_finish(q):
        for third in range(3):
            for phase in range(3):
                for k in range(6 if (q, phase) in RELAYED else 3):
                    ag_copy(q, third, phase, k).wait_send()
            for k in range(4):
                sib_copy(q, third, k).wait_send()

    def find_blocks():
        for n in range(3):
            taken[n] = 0

        @pl.loop(0, DC)
        def _(r):
            for c in range(FC):
                number = r * FC + c
                for n, ids in enumerate((gi, ui, di)):
                    at = jnp.minimum(taken[n], KB - 1)
                    hit = ids[0, at] == number
                    where[n, number] = jnp.where(hit, at, KB)
                    taken[n] = taken[n] + hit.astype(jnp.int32)

    def spread(n, per, store, lo, hi):
        @pl.loop(lo, hi)
        def _(r):
            for c in range(per):
                store(r, c, stage[where[n, r * per + c]])

    def block_rows(r):
        return pl.ds(pl.multiple_of(r * BLK, BLK), BLK)

    def store_gate(r, c, block):
        wgu[c, block_rows(r), pl.ds(0, BLK)] = block

    def store_up(r, c, block):
        wgu[c, block_rows(r), pl.ds(BLK, BLK)] = block

    def store_down(r, c, block):
        wd[block_rows(r), pl.ds(c * BLK, BLK)] = block

    flat = buf.reshape(2, DC, TOK, BLK)

    def rows_of(q, rows):
        return jnp.concatenate([flat[q, j, rows, :] for j in range(DC)], axis=1)

    def forward_cols(lo, hi, start, size, then):
        @pl.loop(lo, hi)
        def _(c):
            for rows in [pl.ds(start, size)]:
                both = jnp.dot(rows_of(0, rows), wgu[c], preferred_element_type=F32)
                gate, up = both[:, :BLK], both[:, BLK:]
                sigma = 1.0 / (1.0 + jnp.exp(-gate))
                swish = gate * sigma
                hid[c, rows, :] = (swish * up).astype(BF16)
                gpre[2 * c, rows, :] = (up * sigma * (1.0 + gate * (1.0 - sigma))).astype(BF16)
                gpre[2 * c + 1, rows, :] = swish.astype(BF16)

            for last, step in then.items():
                pl.when(c == last)(step)

    def backward_cols(start, width):
        for rows in [pl.ds(0, TOK)]:
            w = wd[pl.ds(pl.multiple_of(start * BLK, BLK), width * BLK), :]
            grad = lax.dot_general(
                rows_of(1, rows), w, (((1,), (1,)), ((), ())), preferred_element_type=F32
            )
            for j in range(width):
                piece = grad[:, j * BLK : (j + 1) * BLK]
                for side in range(2):
                    k = 2 * (start + j) + side
                    gpre[k, rows, :] = (gpre[k, rows, :].astype(F32) * piece).astype(BF16)

    def own_rows(ref, *lead):
        runs = []
        for h in range(2):
            for c in range(2):
                at = c * 512 + (z * 4 + h * 2 + ylo) * 32
                rows = pl.ds(pl.multiple_of(at, 32), 32)
                blocks = ref.shape[len(lead)]
                runs.append(
                    jnp.concatenate([ref[(*lead, j, rows)] for j in range(blocks)], axis=1)
                )
        return jnp.concatenate(runs, axis=0)

    def own_backward(start, width):
        w = wd[pl.ds(pl.multiple_of(start * BLK, BLK), width * BLK), :]
        grad = lax.dot_general(
            own_rows(flat, 1), w, (((1,), (1,)), ((), ())), preferred_element_type=F32
        )
        for j in range(width):
            piece = grad[:, j * BLK : (j + 1) * BLK]
            for side in range(2):
                k = 2 * (start + j) + side
                runs = []
                for h in range(2):
                    for c in range(2):
                        at = c * 512 + (z * 4 + h * 2 + ylo) * 32
                        runs.append(gpre[k, pl.ds(pl.multiple_of(at, 32), 32), :])
                slope = jnp.concatenate(runs, axis=0).astype(F32)
                own_g[k] = (slope * piece).astype(BF16)

    def partial_out(o):
        width = 512

        @pl.loop(0, D // width)
        def _(n):
            cols = pl.ds(pl.multiple_of(n * width, width), width)
            if o == 0:
                term = jnp.dot(own_rows(hid), wd[:, cols], preferred_element_type=F32)
            else:
                term = lax.dot_general(
                    jnp.concatenate([own_g[k] for k in range(2 * FC)], axis=1),
                    jnp.concatenate([wgu[c, cols, :] for c in range(FC)], axis=1),
                    (((1,), (1,)), ((), ())),
                    preferred_element_type=F32,
                )
            part[o, :, :, :, :, cols] = term.astype(BF16).reshape(2, 2, 4, 8, width)

    def rs_copy(o, k):
        if k == 0:
            src, dst, to = part.at[o, :, 1 - core], got1.at[o], sibling
        elif k < 4:
            at = moved("x", k)
            src, dst, to = part.at[o, :, core, at["x"]], got2.at[o, k - 1], device(at, core)
        else:
            src, dst, to = mid.at[o, 1 - yhi], got3.at[o], far["y"]
        return pltpu.make_async_remote_copy(
            src_ref=src,
            dst_ref=dst,
            send_sem=rs_send.at[o, k],
            recv_sem=rs_recv.at[o, k],
            device_id=to,
            device_id_type=MESH,
        )

    def rs_one(o):
        rs_copy(o, 0).start()

    def rs_two(o):
        rs_copy(o, 0).wait_recv()
        for h in range(2):
            for w in range(4):
                part[o, h, core, w] = (
                    part[o, h, core, w].astype(F32) + got1[o, h, w].astype(F32)
                ).astype(BF16)
        for k in (2, 1, 3):
            rs_copy(o, k).start()

    def rs_three(o):
        for k in range(1, 4):
            rs_copy(o, k).wait_recv()
        for h in range(2):
            total = part[o, h, core, x].astype(F32)
            for k in range(3):
                total = total + got2[o, k, h].astype(F32)
            mid[o, h] = total.astype(BF16)
        rs_copy(o, 4).start()

    def rs_four(o):
        rs_copy(o, 4).wait_recv()
        total = mid[o, yhi].astype(F32) + got3[o].astype(F32)
        (lo_ref, tg_ref)[o][...] = total.astype(BF16)
        for k in range(5):
            rs_copy(o, k).wait_send()

    def pick_slots():
        @pl.loop(0, CAP)
        def _(v):
            mine = dp * CAP + v
            for n, (ids, slots) in enumerate(((giv, gsv), (uiv, usv), (div, dsv))):
                picks[n, v] = jnp.sum(jnp.where(slots[...] == mine, ids[...] + 1, 0))

    factor = 1.0 / math.sqrt(TOK)

    def block_grad(left, right, weight):
        return (
            lax.dot_general(left, right, (((0,), (0,)), ((), ())), preferred_element_type=F32)
            * weight
        )

    def grads(lo, hi):
        @pl.loop(lo, hi)
        def _(v):
            for n in range(3):
                number = picks[n, v]
                block = jnp.maximum(number - 1, 0)
                weight = jnp.where(number > 0, factor, 0.0)
                if n < 2:
                    left = buf[0, block // FC].reshape(TOK, BLK)
                    right = gpre[2 * (block % FC) + n]
                else:
                    left = hid[block // DC]
                    right = buf[1, block % DC].reshape(TOK, BLK)
                (gg_ref, ug_ref, dg_ref)[n][v] = block_grad(left, right, weight)

    mine, other = core * 512, (1 - core) * 512
    ag_start(0, 0)
    ag_start(1, 0)
    stage[KB] = jnp.zeros((BLK, BLK), BF16)
    for copy in small:
        copy.wait()
    find_blocks()
    ag_wait(0, 0)
    ag_start(0, 1)
    ag_wait(1, 0)
    ag_start(1, 1)
    load(gb_ref).wait()
    spread(0, FC, store_gate, 0, DC)
    load(ub_ref).start()
    ag_wait(0, 1)
    ag_start(0, 2)
    sib_start(0, 0)
    ag_forward(1, 1)
    load(ub_ref).wait()
    spread(1, FC, store_up, 0, DC)
    load(db_ref).start()
    ag_forward(0)
    ag_direct(1, 1)
    ag_far(1, 1)
    ag_start(1, 2)
    load(db_ref).wait()
    spread(2, DC, store_down, 0, 4)
    ag_direct(0)
    sib_start(0, 1)
    sib_start(0, 3)
    sib_start(1, 0)
    spread(2, DC, store_down, 4, FC)
    pick_slots()
    ag_far(0)
    sib_start(0, 2)
    forward_cols(0, 3, pl.multiple_of(mine, 512), 512, {})
    ag_forward(1)
    sib_wait(0)
    forward_cols(0, 3, pl.multiple_of(other, 512), 512, {})

    def cots_direct():
        ag_direct(1)
        sib_start(1, 1)
        sib_start(1, 3)

    def cots_far():
        ag_far(1)
        sib_start(1, 2)

    forward_cols(3, FC, 0, TOK, {3: cots_direct, 5: cots_far})
    partial_out(0)
    rs_one(0)
    sib_wait(1)

    @pl.loop(0, 3)
    def _(c):
        own_backward(2 * c, 2)

    own_backward(FC - 1, 1)
    partial_out(1)
    rs_two(0)
    rs_one(1)

    @pl.loop(0, 3)
    def _(c):
        backward_cols(2 * c, 2)

        @pl.when(c == 1)
        def _():
            rs_two(1)

    rs_three(0)
    backward_cols(FC - 1, 1)
    grads(0, 7)
    rs_three(1)
    rs_four(0)
    grads(7, CAP)
    rs_four(1)
    ag_finish(0)
    ag_finish(1)


def copy_body(*refs):
    sem = refs[10]
    copies = [
        pltpu.make_async_copy(source, target, sem.at[n])
        for n, (source, target) in enumerate(zip(refs[:5], refs[5:10]))
    ]
    for copy in copies:
        copy.start()
    for copy in copies:
        copy.wait()


def local(
    tokens,
    out_grad,
    gate_blocks,
    up_blocks,
    down_blocks,
    gate_index,
    up_index,
    down_index,
    gate_slot,
    up_slot,
    down_slot,
):
    hbm = pl.BlockSpec(memory_space=pl.ANY)
    vmem = pl.BlockSpec(memory_space=pltpu.VMEM)
    rows = jax.ShapeDtypeStruct((8, D), BF16)
    owned = jax.ShapeDtypeStruct((CAP, BLK, BLK), F32)
    shapes = (rows, rows, owned, owned, owned)
    results = pl.pallas_call(
        kernel_body,
        out_shape=tuple(pltpu.VMEM(shape.shape, shape.dtype) for shape in shapes),
        in_specs=[vmem, vmem] + [hbm] * 9,
        out_specs=(vmem,) * 5,
        scratch_shapes=[pltpu.SMEM((1, KB), jnp.int32)] * 3
        + [pltpu.VMEM((1, KB), jnp.int32)] * 6
        + [
            pltpu.SMEM((3, CAP), jnp.int32),
            pltpu.SMEM((3,), jnp.int32),
            pltpu.SMEM((3, NBLK), jnp.int32),
            pltpu.VMEM((2, DC, 2, 4, 4, 4, 8, BLK), BF16),
            pltpu.VMEM((FC, D, 2 * BLK), BF16),
            pltpu.VMEM((FDEV, D), BF16),
            pltpu.VMEM((KB + 1, BLK, BLK), BF16),
            pltpu.VMEM((FC, TOK, BLK), BF16),
            pltpu.VMEM((2 * FC, TOK, BLK), BF16),
            pltpu.VMEM((2 * FC, BLK, BLK), BF16),
            pltpu.VMEM((2, 2, 2, 4, 8, D), BF16),
            pltpu.VMEM((2, 2, 4, 8, D), BF16),
            pltpu.VMEM((2, 3, 2, 8, D), BF16),
            pltpu.VMEM((2, 2, 8, D), BF16),
            pltpu.VMEM((2, 8, D), BF16),
            pltpu.SemaphoreType.DMA((9,)),
            pltpu.SemaphoreType.DMA,
            pltpu.SemaphoreType.DMA((2, 3, 3, 6)),
            pltpu.SemaphoreType.DMA((2, 3, 3, 6)),
            pltpu.SemaphoreType.DMA((2, 3, 4)),
            pltpu.SemaphoreType.DMA((2, 3, 4)),
            pltpu.SemaphoreType.DMA((2, 5)),
            pltpu.SemaphoreType.DMA((2, 5)),
        ],
        compiler_params=pltpu.CompilerParams(
            collective_id=0, has_side_effects=True, vmem_limit_bytes=56 * 1024 * 1024
        ),
    )(
        tokens,
        out_grad,
        gate_blocks,
        up_blocks,
        down_blocks,
        gate_index,
        up_index,
        down_index,
        gate_slot,
        up_slot,
        down_slot,
    )
    lo, tg, gg, ug, dg = pl.pallas_call(
        copy_body,
        out_shape=shapes,
        in_specs=[vmem] * 5,
        out_specs=(hbm,) * 5,
        scratch_shapes=[pltpu.SemaphoreType.DMA((5,))],
    )(*[pltpu.with_memory_space_constraint(r, pltpu.VMEM) for r in results])
    return lo, tg, gg[None], ug[None], dg[None]


def solution(mesh):
    in_specs = (
        P(("dp", "tensor"), None),
        P(("dp", "tensor"), None),
        P("tensor", None, None),
        P("tensor", None, None),
        P("tensor", None, None),
        P("tensor", None),
        P("tensor", None),
        P("tensor", None),
        P("tensor", None),
        P("tensor", None),
        P("tensor", None),
    )
    out_specs = (
        P(("dp", "tensor"), None),
        P(("dp", "tensor"), None),
        P("tensor", "dp", None, None),
        P("tensor", "dp", None, None),
        P("tensor", "dp", None, None),
    )
    return jax.shard_map(local, mesh=mesh, in_specs=in_specs, out_specs=out_specs, check_vma=False)
```

```python
import functools
import math

import jax
import jax.numpy as jnp
from jax import lax
from jax.experimental import pallas as pl
from jax.experimental.pallas import tpu as pltpu
from jax.sharding import PartitionSpec as P

MESH = pl.DeviceIdType.MESH
D = 4096
BLK = 128
DC = 32
FC = 7
FDEV = 896
KB = 112
NBLK = 224
CAP = 17
TOK = 1024
F32 = jnp.float32
BF16 = jnp.bfloat16

THIRDS = ((0, 6, 11), (11, 16, 22), (22, 27, 32))
RELAYED = ((0, 2), (1, 1), (1, 2))
ORDERS = (("x", "y", "z"), ("y", "z", "x"), ("z", "x", "y"))


def kernel_body(
    tok_ref,
    cot_ref,
    gb_ref,
    ub_ref,
    db_ref,
    gi_ref,
    ui_ref,
    di_ref,
    gs_ref,
    us_ref,
    ds_ref,
    lo_ref,
    tg_ref,
    gg_ref,
    ug_ref,
    dg_ref,
    gi,
    ui,
    di,
    giv,
    uiv,
    div,
    gsv,
    usv,
    dsv,
    picks,
    taken,
    where,
    buf,
    wgu,
    wd,
    stage,
    hid,
    gpre,
    own_g,
    part,
    got1,
    got2,
    mid,
    got3,
    in_sem,
    ld_sem,
    ag_send,
    ag_recv,
    sib_send,
    sib_recv,
    rs_send,
    rs_recv,
):
    dp = lax.axis_index("dp")
    tp = lax.axis_index("tensor")
    ylo, z = dp // 4, dp % 4
    x, yhi, core = tp // 4, (tp // 2) % 2, tp % 2
    y = yhi * 2 + ylo
    here = {"x": x, "y": y, "z": z}

    def device(at, c):
        return (
            (at["y"] % 2) * 4 + at["z"],
            at["x"] * 4 + (at["y"] // 2) * 2 + c,
        )

    def moved(axis, step):
        at = dict(here)
        at[axis] = (here[axis] + step) % 4
        return at

    right = {a: device(moved(a, 1), core) for a in "xyz"}
    left = {a: device(moved(a, 3), core) for a in "xyz"}
    far = {a: device(moved(a, 2), core) for a in "xyz"}
    sibling = device(here, 1 - core)

    small = [
        pltpu.make_async_copy(src, dst, in_sem.at[n])
        for n, (src, dst) in enumerate(
            (
                (gi_ref, gi),
                (ui_ref, ui),
                (di_ref, di),
                (gi_ref, giv),
                (ui_ref, uiv),
                (di_ref, div),
                (gs_ref, gsv),
                (us_ref, usv),
                (ds_ref, dsv),
            )
        )
    ]

    def load(src):
        return pltpu.make_async_copy(src, stage.at[pl.ds(0, KB)], ld_sem)

    barrier = pltpu.get_barrier_semaphore()
    partners = list(right.values()) + list(left.values()) + list(far.values()) + [sibling]
    for other in partners:
        pl.semaphore_signal(barrier, inc=1, device_id=other, device_id_type=MESH)
    for copy in small:
        copy.start()
    load(gb_ref).start()
    for j in range(DC):
        cols = pl.ds(j * BLK, BLK)
        buf[0, j, core, z, y, x] = tok_ref[:, cols]
        buf[1, j, core, z, y, x] = cot_ref[:, cols]
    pl.semaphore_wait(barrier, len(partners))

    def region(q, third, phase, along, lo, hi):
        axes = ORDERS[third]
        idx = []
        for a in ("z", "y", "x"):
            if a in axes[:phase]:
                idx.append(slice(None))
            elif a == axes[phase]:
                idx.append(along)
            else:
                idx.append(here[a])
        return buf.at[(q, pl.ds(lo, hi - lo), core, *idx)]

    def ag_copy(q, third, phase, k):
        lo, mid_col, hi = THIRDS[third]
        axis = ORDERS[third][phase]
        own = here[axis]
        if (q, phase) not in RELAYED:
            along, cols, to = own, (lo, hi), (right, left, far)[k]
        else:
            along, cols, to = (
                (own, (lo, mid_col), right),
                (own, (mid_col, hi), left),
                (own, (mid_col, hi), right),
                (own, (lo, mid_col), left),
                ((own + 3) % 4, (lo, mid_col), right),
                ((own + 1) % 4, (mid_col, hi), left),
            )[k]
        ref = region(q, third, phase, along, *cols)
        return pltpu.make_async_remote_copy(
            src_ref=ref,
            dst_ref=ref,
            send_sem=ag_send.at[q, third, phase, k],
            recv_sem=ag_recv.at[q, third, phase, k],
            device_id=to[axis],
            device_id_type=MESH,
        )

    def sib_copy(q, third, k):
        lo, _, hi = THIRDS[third]
        axis = ORDERS[third][2]
        ref = region(q, third, 2, (here[axis] + k) % 4, lo, hi)
        return pltpu.make_async_remote_copy(
            src_ref=ref,
            dst_ref=ref,
            send_sem=sib_send.at[q, third, k],
            recv_sem=sib_recv.at[q, third, k],
            device_id=sibling,
            device_id_type=MESH,
        )

    def ag_start(q, phase):
        for k in range(4 if (q, phase) in RELAYED else 3):
            for third in range(3):
                ag_copy(q, third, phase, k).start()

    def ag_forward(q, phase=2):
        for third in range(3):
            ag_copy(q, third, phase, 0).wait_recv()
            ag_copy(q, third, phase, 4).start()
            ag_copy(q, third, phase, 1).wait_recv()
            ag_copy(q, third, phase, 5).start()

    def ag_direct(q, phase=2):
        for third in range(3):
            ag_copy(q, third, phase, 2).wait_recv()
            ag_copy(q, third, phase, 3).wait_recv()

    def ag_far(q, phase=2):
        for third in range(3):
            ag_copy(q, third, phase, 4).wait_recv()
            ag_copy(q, third, phase, 5).wait_recv()

    def ag_next(q, phase):
        for third in range(3):
            for k in range(3):
                ag_copy(q, third, phase, k).wait_recv()
            for k in range(4 if (q, phase + 1) in RELAYED else 3):
                ag_copy(q, third, phase + 1, k).start()

    def ag_last(q):
        for third in range(3):
            ag_copy(q, third, 2, 4).wait_recv()
            ag_copy(q, third, 2, 5).wait_recv()
            sib_copy(q, third, 2).start()

    def ag_sides(q):
        for third in range(3):
            ag_copy(q, third, 2, 2).wait_recv()
            ag_copy(q, third, 2, 3).wait_recv()
            sib_copy(q, third, 1).start()
            sib_copy(q, third, 3).start()

    def sib_start(q, k):
        for third in range(3):
            sib_copy(q, third, k).start()

    def sib_wait(q):
        for third in range(3):
            for k in range(4):
                sib_copy(q, third, k).wait_recv()

    def ag_finish(q):
        for third in range(3):
            for phase in range(3):
                for k in range(6 if (q, phase) in RELAYED else 3):
                    ag_copy(q, third, phase, k).wait_send()
            for k in range(4):
                sib_copy(q, third, k).wait_send()

    def find_blocks():
        for n in range(3):
            taken[n] = 0

        @pl.loop(0, DC)
        def _(r):
            for c in range(FC):
                number = r * FC + c
                for n, ids in enumerate((gi, ui, di)):
                    at = jnp.minimum(taken[n], KB - 1)
                    hit = ids[0, at] == number
                    where[n, number] = jnp.where(hit, at, KB)
                    taken[n] = taken[n] + hit.astype(jnp.int32)

    def spread(n, per, store, lo, hi):
        @pl.loop(lo, hi)
        def _(r):
            for c in range(per):
                store(r, c, stage[where[n, r * per + c]])

    def block_rows(r):
        return pl.ds(pl.multiple_of(r * BLK, BLK), BLK)

    def store_gate(r, c, block):
        wgu[c, block_rows(r), pl.ds(0, BLK)] = block

    def store_up(r, c, block):
        wgu[c, block_rows(r), pl.ds(BLK, BLK)] = block

    def store_down(r, c, block):
        wd[block_rows(r), pl.ds(c * BLK, BLK)] = block

    flat = buf.reshape(2, DC, TOK, BLK)

    def rows_of(q, rows):
        return jnp.concatenate([flat[q, j, rows, :] for j in range(DC)], axis=1)

    def forward_cols(lo, hi, start, size, then):
        @pl.loop(lo, hi)
        def _(c):
            for rows in [pl.ds(start, size)]:
                both = jnp.dot(rows_of(0, rows), wgu[c], preferred_element_type=F32)
                gate, up = both[:, :BLK], both[:, BLK:]
                sigma = 1.0 / (1.0 + jnp.exp(-gate))
                swish = gate * sigma
                hid[c, rows, :] = (swish * up).astype(BF16)
                gpre[2 * c, rows, :] = (up * sigma * (1.0 + gate * (1.0 - sigma))).astype(BF16)
                gpre[2 * c + 1, rows, :] = swish.astype(BF16)

            for last, step in then.items():
                pl.when(c == last)(step)

    def backward_cols(start, width):
        for rows in [pl.ds(0, TOK)]:
            w = wd[pl.ds(pl.multiple_of(start * BLK, BLK), width * BLK), :]
            grad = lax.dot_general(
                rows_of(1, rows), w, (((1,), (1,)), ((), ())), preferred_element_type=F32
            )
            for j in range(width):
                piece = grad[:, j * BLK : (j + 1) * BLK]
                for side in range(2):
                    k = 2 * (start + j) + side
                    gpre[k, rows, :] = (gpre[k, rows, :].astype(F32) * piece).astype(BF16)

    def own_rows(ref, *lead):
        runs = []
        for h in range(2):
            for c in range(2):
                at = c * 512 + (z * 4 + h * 2 + ylo) * 32
                rows = pl.ds(pl.multiple_of(at, 32), 32)
                blocks = ref.shape[len(lead)]
                runs.append(
                    jnp.concatenate([ref[(*lead, j, rows)] for j in range(blocks)], axis=1)
                )
        return jnp.concatenate(runs, axis=0)

    def own_backward(start, width):
        w = wd[pl.ds(pl.multiple_of(start * BLK, BLK), width * BLK), :]
        grad = lax.dot_general(
            own_rows(flat, 1), w, (((1,), (1,)), ((), ())), preferred_element_type=F32
        )
        for j in range(width):
            piece = grad[:, j * BLK : (j + 1) * BLK]
            for side in range(2):
                k = 2 * (start + j) + side
                runs = []
                for h in range(2):
                    for c in range(2):
                        at = c * 512 + (z * 4 + h * 2 + ylo) * 32
                        runs.append(gpre[k, pl.ds(pl.multiple_of(at, 32), 32), :])
                slope = jnp.concatenate(runs, axis=0).astype(F32)
                own_g[k] = (slope * piece).astype(BF16)

    def partial_out(o):
        width = 1024

        @pl.loop(0, D // width)
        def _(n):
            cols = pl.ds(pl.multiple_of(n * width, width), width)
            if o == 0:
                term = jnp.dot(own_rows(hid), wd[:, cols], preferred_element_type=F32)
            else:
                term = lax.dot_general(
                    jnp.concatenate([own_g[k] for k in range(2 * FC)], axis=1),
                    jnp.concatenate([wgu[c, cols, :] for c in range(FC)], axis=1),
                    (((1,), (1,)), ((), ())),
                    preferred_element_type=F32,
                )
            part[o, :, :, :, :, cols] = term.astype(BF16).reshape(2, 2, 4, 8, width)

    def rs_copy(o, k):
        if k == 0:
            src, dst, to = part.at[o, :, 1 - core], got1.at[o], sibling
        elif k < 4:
            at = moved("x", k)
            src, dst, to = part.at[o, :, core, at["x"]], got2.at[o, k - 1], device(at, core)
        else:
            src, dst, to = mid.at[o, 1 - yhi], got3.at[o], far["y"]
        return pltpu.make_async_remote_copy(
            src_ref=src,
            dst_ref=dst,
            send_sem=rs_send.at[o, k],
            recv_sem=rs_recv.at[o, k],
            device_id=to,
            device_id_type=MESH,
        )

    def rs_one(o):
        rs_copy(o, 0).start()

    def rs_two(o):
        rs_copy(o, 0).wait_recv()
        for h in range(2):
            for w in range(4):
                part[o, h, core, w] = (
                    part[o, h, core, w].astype(F32) + got1[o, h, w].astype(F32)
                ).astype(BF16)
        for k in (2, 1, 3):
            rs_copy(o, k).start()

    def rs_three(o):
        for k in range(1, 4):
            rs_copy(o, k).wait_recv()
        for h in range(2):
            total = part[o, h, core, x].astype(F32)
            for k in range(3):
                total = total + got2[o, k, h].astype(F32)
            mid[o, h] = total.astype(BF16)
        rs_copy(o, 4).start()

    def rs_four(o):
        rs_copy(o, 4).wait_recv()
        total = mid[o, yhi].astype(F32) + got3[o].astype(F32)
        (lo_ref, tg_ref)[o][...] = total.astype(BF16)
        for k in range(5):
            rs_copy(o, k).wait_send()

    def pick_slots():
        @pl.loop(0, CAP)
        def _(v):
            mine = dp * CAP + v
            for n, (ids, slots) in enumerate(((giv, gsv), (uiv, usv), (div, dsv))):
                picks[n, v] = jnp.sum(jnp.where(slots[...] == mine, ids[...] + 1, 0))

    factor = 1.0 / math.sqrt(TOK)

    def block_grad(left, right, weight):
        return (
            lax.dot_general(left, right, (((0,), (0,)), ((), ())), preferred_element_type=F32)
            * weight
        )

    def grads(lo, hi):
        @pl.loop(lo, hi)
        def _(v):
            for n in range(3):
                number = picks[n, v]
                block = jnp.maximum(number - 1, 0)
                weight = jnp.where(number > 0, factor, 0.0)
                if n < 2:
                    left = buf[0, block // FC].reshape(TOK, BLK)
                    right = gpre[2 * (block % FC) + n]
                else:
                    left = hid[block // DC]
                    right = buf[1, block % DC].reshape(TOK, BLK)
                (gg_ref, ug_ref, dg_ref)[n][v] = block_grad(left, right, weight)

    mine, other = core * 512, (1 - core) * 512
    ag_start(0, 0)
    ag_start(1, 0)
    stage[KB] = jnp.zeros((BLK, BLK), BF16)
    for copy in small:
        copy.wait()
    find_blocks()
    ag_next(0, 0)
    ag_next(1, 0)
    load(gb_ref).wait()
    spread(0, FC, store_gate, 0, DC)
    load(ub_ref).start()
    ag_next(0, 1)
    sib_start(0, 0)
    ag_forward(1, 1)
    load(ub_ref).wait()
    spread(1, FC, store_up, 0, DC)
    load(db_ref).start()
    ag_forward(0)
    ag_direct(1, 1)
    ag_far(1, 1)
    ag_start(1, 2)
    load(db_ref).wait()
    spread(2, DC, store_down, 0, 4)
    ag_sides(0)
    sib_start(1, 0)
    spread(2, DC, store_down, 4, FC)
    pick_slots()
    ag_last(0)
    forward_cols(0, 3, pl.multiple_of(mine, 512), 512, {})
    ag_forward(1)
    sib_wait(0)
    forward_cols(0, 3, pl.multiple_of(other, 512), 512, {})

    def cots_direct():
        ag_sides(1)

    def cots_far():
        ag_last(1)

    forward_cols(3, FC, 0, TOK, {3: cots_direct, 5: cots_far})
    partial_out(0)
    rs_one(0)
    sib_wait(1)

    @pl.loop(0, 3)
    def _(c):
        own_backward(2 * c, 2)

    own_backward(FC - 1, 1)
    partial_out(1)
    rs_two(0)
    rs_one(1)

    @pl.loop(0, 3)
    def _(c):
        backward_cols(2 * c, 2)

        @pl.when(c == 1)
        def _():
            rs_two(1)

    rs_three(0)
    backward_cols(FC - 1, 1)
    grads(0, 7)
    rs_three(1)
    rs_four(0)
    grads(7, CAP)
    rs_four(1)
    ag_finish(0)
    ag_finish(1)


def copy_body(*refs):
    sem = refs[10]
    copies = [
        pltpu.make_async_copy(source, target, sem.at[n])
        for n, (source, target) in enumerate(zip(refs[:5], refs[5:10]))
    ]
    for copy in copies:
        copy.start()
    for copy in copies:
        copy.wait()


def local(
    tokens,
    out_grad,
    gate_blocks,
    up_blocks,
    down_blocks,
    gate_index,
    up_index,
    down_index,
    gate_slot,
    up_slot,
    down_slot,
):
    hbm = pl.BlockSpec(memory_space=pl.ANY)
    vmem = pl.BlockSpec(memory_space=pltpu.VMEM)
    rows = jax.ShapeDtypeStruct((8, D), BF16)
    owned = jax.ShapeDtypeStruct((CAP, BLK, BLK), F32)
    shapes = (rows, rows, owned, owned, owned)
    results = pl.pallas_call(
        kernel_body,
        out_shape=tuple(pltpu.VMEM(shape.shape, shape.dtype) for shape in shapes),
        in_specs=[vmem, vmem] + [hbm] * 9,
        out_specs=(vmem,) * 5,
        scratch_shapes=[pltpu.SMEM((1, KB), jnp.int32)] * 3
        + [pltpu.VMEM((1, KB), jnp.int32)] * 6
        + [
            pltpu.SMEM((3, CAP), jnp.int32),
            pltpu.SMEM((3,), jnp.int32),
            pltpu.SMEM((3, NBLK), jnp.int32),
            pltpu.VMEM((2, DC, 2, 4, 4, 4, 8, BLK), BF16),
            pltpu.VMEM((FC, D, 2 * BLK), BF16),
            pltpu.VMEM((FDEV, D), BF16),
            pltpu.VMEM((KB + 1, BLK, BLK), BF16),
            pltpu.VMEM((FC, TOK, BLK), BF16),
            pltpu.VMEM((2 * FC, TOK, BLK), BF16),
            pltpu.VMEM((2 * FC, BLK, BLK), BF16),
            pltpu.VMEM((2, 2, 2, 4, 8, D), BF16),
            pltpu.VMEM((2, 2, 4, 8, D), BF16),
            pltpu.VMEM((2, 3, 2, 8, D), BF16),
            pltpu.VMEM((2, 2, 8, D), BF16),
            pltpu.VMEM((2, 8, D), BF16),
            pltpu.SemaphoreType.DMA((9,)),
            pltpu.SemaphoreType.DMA,
            pltpu.SemaphoreType.DMA((2, 3, 3, 6)),
            pltpu.SemaphoreType.DMA((2, 3, 3, 6)),
            pltpu.SemaphoreType.DMA((2, 3, 4)),
            pltpu.SemaphoreType.DMA((2, 3, 4)),
            pltpu.SemaphoreType.DMA((2, 5)),
            pltpu.SemaphoreType.DMA((2, 5)),
        ],
        compiler_params=pltpu.CompilerParams(
            collective_id=0, has_side_effects=True, vmem_limit_bytes=56 * 1024 * 1024
        ),
    )(
        tokens,
        out_grad,
        gate_blocks,
        up_blocks,
        down_blocks,
        gate_index,
        up_index,
        down_index,
        gate_slot,
        up_slot,
        down_slot,
    )
    lo, tg, gg, ug, dg = pl.pallas_call(
        copy_body,
        out_shape=shapes,
        in_specs=[vmem] * 5,
        out_specs=(hbm,) * 5,
        scratch_shapes=[pltpu.SemaphoreType.DMA((5,))],
    )(*[pltpu.with_memory_space_constraint(r, pltpu.VMEM) for r in results])
    return lo, tg, gg[None], ug[None], dg[None]


def solution(mesh):
    in_specs = (
        P(("dp", "tensor"), None),
        P(("dp", "tensor"), None),
        P("tensor", None, None),
        P("tensor", None, None),
        P("tensor", None, None),
        P("tensor", None),
        P("tensor", None),
        P("tensor", None),
        P("tensor", None),
        P("tensor", None),
        P("tensor", None),
    )
    out_specs = (
        P(("dp", "tensor"), None),
        P(("dp", "tensor"), None),
        P("tensor", "dp", None, None),
        P("tensor", "dp", None, None),
        P("tensor", "dp", None, None),
    )
    return jax.shard_map(local, mesh=mesh, in_specs=in_specs, out_specs=out_specs, check_vma=False)
```
